32 devices in a mesh: site: 32 (over z, y, x, core).
Axes of the slice: x: 2, y: 2, z: 4, core: 2. Of those that a mesh axis runs over, the one named last changes fastest.
Arguments:
- sites: float32 [32, 2, 12, 128, 128], P('site'), may hold values from -0.5 to 0.5
- sector_sizes: int32 [32, 12], P('site'), may hold values from 64 to 128, as said below
- charge_steps: int32 [32], P('site'), may hold values from 0 to 1
- kept_counts: int32 [32, 12], P('site'), may hold values from 64 to 128, as said below
- gates: float32 [32, 6], P('site'), may hold values from 0.4 to 1.2
- sketches: float32 [32, 12, 256, 128], P('site'), may hold values from -0.375 to 0.375
Outputs:
- new_sites: float32 [32, 2, 12, 128, 128], P('site')
- totals: float32 [2], replicated
The draws below stay inside these ranges and needn't reach their ends.
Inputs may be any that keep to these rules, and one draw needn't show every extreme that they name: `sector_sizes`: every sector holds at least 64 states; each bond has one sector of exactly 128 states. kept_counts[i, c] is at least 64 and at most sector_sizes[(i + 1) mod 32, c]; on each bond the sector of 128 states keeps all of them.
All inputs are finite; a program needn't handle non-finite values.
Results may differ from the reference program's by a relative error of at most 0.0003.
Values sent between devices are 32-bit elements; how exact they have to be, the bound alone decides.
A program may use at most 64 MiB of HBM per device.

```python
import jax
import jax.numpy as jnp
from jax import lax

NSEC = 12
SMAX = 128
STEPS = 4
SITES = 32


def label_tables(key):
    sizes = jax.random.randint(jax.random.fold_in(key, 101), (SITES, NSEC), SMAX // 2, SMAX + 1)
    full_at = jax.random.randint(jax.random.fold_in(key, 102), (SITES,), 0, NSEC)
    sectors = jnp.arange(NSEC)[None, :]
    sizes = jnp.where(sectors == full_at[:, None], SMAX, sizes)
    following = jnp.roll(sizes, -1, axis=0)
    kept = jax.random.randint(jax.random.fold_in(key, 103), (SITES, NSEC), SMAX // 2, following + 1)
    whole_at = jnp.roll(full_at, -1)
    kept = jnp.where(sectors == whole_at[:, None], following, kept)
    return (sizes.astype(jnp.int32), kept.astype(jnp.int32))


def draw_sector_sizes(key, part):
    return label_tables(key)[0]


def draw_kept_counts(key, part):
    return label_tables(key)[1]


def touch_ends(values, rng, smallest, largest):
    longest = values.shape.index(max(values.shape))
    spots = []
    for shift in (0, 1):
        where = [jax.random.randint(jax.random.fold_in(rng, axis), (), 0, length) for axis, length in enumerate(values.shape)]
        where[longest] = (where[longest] + shift) % values.shape[longest]
        spots.append(tuple(where))
    return values.at[spots[0]].set(smallest).at[spots[1]].set(largest)


def level_of(own_key, shape, pieces, smallest, top_value):
    level, own = 1.0, jax.random.fold_in(own_key, 6)
    for position, shards_of in pieces:
        draws = jnp.exp(jax.random.uniform(jax.random.fold_in(own, position), (shards_of,), jnp.float32, smallest / len(pieces), top_value / len(pieces)))
        level = level * jnp.repeat(draws, shape[position] // shards_of).reshape([-1 if axis == position else 1 for axis in range(len(shape))])
    return level


def scatter_about(stream_key, extent, scale, most, cuts=(), kind=jnp.bfloat16):
    values = jax.random.normal(stream_key, extent, jnp.float32) * scale
    if len(cuts) > 0:
        values = level_of(stream_key, extent, cuts, -0.22, 0.18) * values
    return jnp.clip(values, min=-most, max=most).astype(kind)


def setup_inputs(seed: int = 0) -> dict:
    key_of = jax.random.split(jax.random.key(seed), 7)
    return {
        "sites": scatter_about(key_of[0], (SITES, 2, NSEC, SMAX, SMAX), SMAX ** -0.5, 0.5, ((0, 32),), jnp.float32),
        "sector_sizes": draw_sector_sizes(jax.random.fold_in(key_of[6], 71), 0),
        "charge_steps": touch_ends(jax.random.randint(key_of[2], (SITES,), 0, 2), jax.random.fold_in(key_of[2], 1), 0, 1).astype(jnp.int32),
        "kept_counts": draw_kept_counts(jax.random.fold_in(key_of[6], 71), 0),
        "gates": jnp.clip(0.4 + 0.800000042 * jax.random.uniform(key_of[4], (SITES, 6), jnp.float32) ** level_of(key_of[4], (SITES, 6), ((0, 32),), -0.2, 0.2), 0.4, 1.2),
        "sketches": scatter_about(key_of[5], (SITES, NSEC, 2 * SMAX, SMAX), (2 * SMAX) ** -0.5, 0.375, ((0, 32),), jnp.float32),
    }


def sector_index(count, shift, extra):
    return ((jnp.arange(count, dtype=jnp.int32) + extra - shift) % count).astype(jnp.int32)

def theta_blocks(left, right, shift, gate):
    count = left.shape[1]
    lower_mid = sector_index(count, shift, 0)
    upper_mid = sector_index(count, shift, 1)

    def product(first, second):
        return jnp.einsum('lam,lmb->lab', first, second, precision=lax.Precision.HIGHEST)
    zero_zero = product(left[0], right[0][lower_mid])
    zero_one = product(left[0], right[1][lower_mid])
    one_zero = product(left[1], right[0][upper_mid])
    one_one = product(left[1], right[1][upper_mid])
    mixed_up = gate[2] * zero_one + gate[3] * one_zero
    mixed_down = gate[4] * zero_one + gate[5] * one_zero
    return (gate[0] * zero_zero, mixed_up, mixed_down, gate[1] * one_one)

def split_sectors(blocks, middle, shift, sketch, kept):
    count = blocks[0].shape[0]
    width = blocks[0].shape[-1]
    top = ((middle + shift) % count).astype(jnp.int32)
    bottom = ((middle + shift - 1) % count).astype(jnp.int32)
    upper = jnp.concatenate([blocks[0][top], blocks[1][top]], axis=2)
    lower = jnp.concatenate([blocks[2][bottom], blocks[3][bottom]], axis=2)
    matrix = jnp.concatenate([upper, lower], axis=1)
    used = (jnp.arange(width, dtype=jnp.int32)[None, :] < kept[:, None]).astype(jnp.float32)
    sample = jnp.einsum('kij,kjs->kis', matrix, sketch * used[:, None, :], precision=lax.Precision.HIGHEST)
    gram = jnp.einsum('kis,kit->kst', sample, sample, precision=lax.Precision.HIGHEST)
    diag_sum = lax.optimization_barrier(jnp.sum(sample * sample, axis=(1, 2)))
    ridge = 0.001 * diag_sum / kept.astype(jnp.float32) + 1e-06
    identity = jnp.eye(width, dtype=jnp.float32)[None]
    gram = gram + identity * ridge[:, None, None] + identity * (1.0 - used)[:, None, :]
    factor = jnp.linalg.cholesky(gram)
    solved = jax.scipy.linalg.solve_triangular(factor, jnp.swapaxes(sample, 1, 2), lower=True)
    basis = jnp.swapaxes(solved, 1, 2)
    reduced = jnp.einsum('kis,kij->ksj', basis, matrix, precision=lax.Precision.HIGHEST)
    return (basis, reduced, jnp.sum(matrix * matrix), jnp.sum(reduced * reduced))

def rebuild(basis, reduced, shift, weight):
    count = basis.shape[0]
    width = basis.shape[2]
    left_new = jnp.stack([basis[sector_index(count, shift, 0), :width], basis[sector_index(count, shift, 1), width:]])
    right_new = jnp.stack([reduced[..., :width], reduced[..., width:]]) / jnp.sqrt(weight)
    return (left_new, right_new)

def bond_update(left, right, shift, gate, sketch, kept):
    blocks = theta_blocks(left, right, shift, gate)
    middle = jnp.arange(left.shape[1], dtype=jnp.int32)
    basis, reduced, total, weight = split_sectors(blocks, middle, shift, sketch, kept)
    left_new, right_new = rebuild(basis, reduced, shift, weight)
    return (left_new, right_new, 1.0 - weight / total, jnp.log(total))

def mask_sites(sites, sizes, steps):
    count = sites.shape[2]
    width = sites.shape[-1]
    following = jnp.roll(sizes, -1, axis=0)
    states = jnp.arange(width, dtype=jnp.int32)
    rows = states[None, None, :] < sizes[:, :, None]
    masks = []
    for phys in range(2):
        target = ((jnp.arange(count, dtype=jnp.int32)[None, :] + phys - steps[:, None]) % count).astype(jnp.int32)
        col_size = jnp.take_along_axis(following, target, axis=1)
        cols = states[None, None, :] < col_size[:, :, None]
        masks.append(rows[:, :, :, None] & cols[:, :, None, :])
    mask = jnp.stack(masks, axis=1)
    return sites * mask.astype(jnp.float32)

def reference(sites, sector_sizes, charge_steps, kept_counts, gates, sketches):
    state = mask_sites(sites, sector_sizes, charge_steps)
    chain = state.shape[0]
    discarded = jnp.zeros((), jnp.float32)
    log_total = jnp.zeros((), jnp.float32)
    for sweep in range(2 * STEPS):
        parity = sweep % 2
        pairs = chain // 2 - parity
        stop = parity + 2 * pairs
        items = (state[parity:stop:2], state[parity + 1:stop + 1:2], charge_steps[parity:stop:2], gates[parity:stop:2], sketches[parity:stop:2], kept_counts[parity:stop:2])

        def one_bond(item):
            return bond_update(item[0], item[1], item[2], item[3], item[4], item[5])
        new_left, new_right, lost, logs = lax.map(one_bond, items)
        state = state.at[parity:stop:2].set(new_left)
        state = state.at[parity + 1:stop + 1:2].set(new_right)
        discarded = discarded + jnp.sum(lost)
        log_total = log_total + jnp.sum(logs)
    return (state, jnp.stack([discarded, log_total]))
```

```python
import functools

import jax
import jax.numpy as jnp
from jax import lax
from jax.experimental import pallas as pl
from jax.experimental.pallas import tpu as pltpu
from jax.sharding import PartitionSpec as P

STEPS = 4
HI = lax.Precision.HIGHEST
MESH = pl.DeviceIdType.MESH
OWN, IN, OUT = 0, 1, 2


def mm(a, b, ca=1, cb=0):
    return lax.dot_general(
        a, b, (((ca,), (cb,)), ((), ())), precision=HI, preferred_element_type=jnp.float32
    )


def inverse_factors(w_ref, z_ref, n, width):
    strip = 32
    lanes = lax.broadcasted_iota(jnp.int32, (1, 8, width), 2)
    subs = lax.broadcasted_iota(jnp.int32, (1, 8, width), 1)
    for b in range(width // strip):
        r0 = b * strip
        groups = strip // 8
        ps = [w_ref[:, r0 + 8 * g : r0 + 8 * g + 8, :] for g in range(groups)]
        if b == 0:
            zs = [
                jnp.broadcast_to((lanes == subs + 8 * g).astype(jnp.float32), ps[0].shape)
                for g in range(groups)
            ]
        else:
            zs = [z_ref[:, r0 + 8 * g : r0 + 8 * g + 8, :] for g in range(groups)]
        for q in range(groups):
            vs = [
                [
                    jnp.broadcast_to(
                        ps[g][:, :, r0 + 8 * q + t : r0 + 8 * q + t + 1], ps[g].shape
                    )
                    if g >= q
                    else None
                    for g in range(groups)
                ]
                for t in range(8)
            ]
            root = jnp.zeros_like(ps[q])
            for t in range(8):
                piv = vs[t][q][:, t : t + 1, :]
                inv = lax.rsqrt(piv)
                inv = inv * (1.5 - 0.5 * piv * inv * inv)
                inv2 = inv * inv
                root = jnp.where(subs == t, inv, root)
                below = jnp.where(subs > t, vs[t][q], 0.0)

                def eliminate(rows):
                    scaled = rows[q][:, t : t + 1, :] * inv2
                    out = list(rows)
                    if t < 7:
                        out[q] = rows[q] - below * scaled
                    for g in range(q + 1, groups):
                        out[g] = rows[g] - vs[t][g] * scaled
                    return out

                ps = eliminate(ps)
                zs = eliminate(zs)
                for t2 in range(t + 1, 8):
                    vs[t2] = eliminate(vs[t2])
            ps[q] = ps[q] * root
            zs[q] = zs[q] * root
        for g in range(groups):
            z_ref[:, r0 + 8 * g : r0 + 8 * g + 8, :] = zs[g]
            w_ref[:, r0 + 8 * g : r0 + 8 * g + 8, :] = ps[g]
        r1 = r0 + strip
        if r1 < width:
            rest = width - r1

            def trail(k, carry, r0=r0, r1=r1, rest=rest, b=b):
                pk = w_ref[k, r0:r1, :]
                zk = z_ref[k, r0:r1, :]
                both = mm(pk, jnp.concatenate([pk, zk], axis=1), 0, 0)[r1:]
                w_ref[k, r1:, :] = w_ref[k, r1:, :] - both[:, :width]
                if b == 0:
                    ri = lax.broadcasted_iota(jnp.int32, (rest, width), 0) + r1
                    ci = lax.broadcasted_iota(jnp.int32, (rest, width), 1)
                    old = (ri == ci).astype(jnp.float32)
                else:
                    old = z_ref[k, r1:, :]
                z_ref[k, r1:, :] = old - both[:, width:]
                return carry

            lax.fori_loop(0, n, trail, 0, unroll=True)


def chain_kernel(
    n, width, chain,
    table, gate_tile, sites, sketches,
    out, sums,
    sites_v, sk_v, tab_v, tab_s, gate_v, kept_s, sk_out, sk_b,
    big, st_own, st_in, all_v, acc, prev_w, mat, smp, w_ref, z_ref, tot, wgt,
    load_sem, bar_send, bar_recv, gate_sem, sk_send, sk_recv, tr_send, tr_recv,
    ed_send, ed_recv, st_send, st_recv, sum_send, sum_recv,
):
    f32 = jnp.float32
    count = 2 * n
    sweeps = 2 * STEPS
    me = lax.axis_index("site")
    half = lax.rem(me, 2)
    odd = half == 1
    even_partner = me + 1 - 2 * half
    odd_partner = lax.rem(me - 1 + 2 * half + chain, chain)
    after_me = lax.rem(me + 1, chain)
    before_me = lax.rem(me + chain - 1, chain)

    def kk(i):
        return i + half * (n - 1 - 2 * i)

    def jj(m):
        return m + half * (n - 2 * m)

    load_sites = pltpu.make_async_copy(sites, sites_v, load_sem.at[0])
    load_sk = pltpu.make_async_copy(sketches, sk_v, load_sem.at[1])
    load_sites.start()
    load_sk.start()

    barrier = pltpu.get_barrier_semaphore()

    def greet(off, carry):
        pl.semaphore_signal(
            barrier, inc=1, device_id=(lax.rem(me + off, chain),), device_id_type=MESH
        )
        return carry

    lax.fori_loop(1, chain, greet, 0)
    pl.semaphore_wait(barrier, chain - 1)

    def remote(src, dst, send, recv, to):
        return pltpu.make_async_remote_copy(
            src_ref=src, dst_ref=dst, send_sem=send, recv_sem=recv,
            device_id=(to,), device_id_type=MESH,
        )

    def table_copy(off):
        return remote(
            table, tab_v.at[me], bar_send.at[off], bar_recv.at[off], lax.rem(me + off, chain)
        )

    def begin_table(off, carry):
        table_copy(off).start()
        return carry

    def finish_table(off, carry):
        table_copy(off).wait()
        return carry

    lax.fori_loop(1, chain, begin_table, 0)
    gate_copy = remote(gate_tile, gate_v.at[1], gate_sem.at[0], gate_sem.at[1], after_me)
    gate_copy.start()
    tab_v[me] = table[...]
    gate_v[0] = gate_tile[...]
    lax.fori_loop(1, chain, finish_table, 0)
    to_scalar = pltpu.make_async_copy(tab_v, tab_s, load_sem.at[2])
    to_scalar.start()
    to_scalar.wait()

    def add_step(d, total):
        return total + jnp.where(d < me, tab_s[d, 0, 2 * count], 0)

    before = lax.rem(lax.fori_loop(0, chain, add_step, jnp.int32(0)), count)
    step = tab_s[me, 0, 2 * count]
    after = before + step

    def wrap(x):
        return lax.rem(x + 2 * count, count)

    row_ids = lax.broadcasted_iota(jnp.int32, (width, width), 0)
    col_ids = lax.broadcasted_iota(jnp.int32, (width, width), 1)
    col_row = lax.broadcasted_iota(jnp.int32, (1, width), 1)
    eye = row_ids == col_ids

    load_sites.wait()

    def block(charge, p):
        label = wrap(charge - before - half * p)
        target = wrap(label + p - step)
        rows = tab_s[me, 0, label]
        cols = tab_s[after_me, 0, target]
        keep = (row_ids < rows) & (col_ids < cols)
        return jnp.where(keep, sites_v[p * count + label], 0.0)

    theirs = (1 - half) * n

    def trav_copy(t, k, to):
        return remote(
            big.at[OUT, t, k], big.at[IN, t, k], tr_send.at[t, k], tr_recv.at[t, k], to
        )

    def edge_copy(t, kind, src, k, to):
        return remote(
            big.at[src, t, k], big.at[kind, t, n], ed_send.at[t, kind], ed_recv.at[t, kind], to
        )

    def stat_copy(t, kind, to):
        return remote(
            st_own.at[t], st_in.at[kind, t], st_send.at[t, kind], st_recv.at[t, kind], to
        )

    for i in range(n):
        k = n - 1 - kk(i)
        for p in range(2):
            big[OUT, 0, k, p] = block(theirs + k, p)
        trav_copy(0, k, even_partner).start()
    for i in range(n):
        k = n - 1 - i
        for p in range(2):
            big[OWN, 0, k, p] = block(half * n + k, p)
    for p in range(2):
        big[OWN, 0, n, p] = big[OUT, 0, kk(n - 1), p]
    edge_copy(0, 1, OWN, kk(n - 1), even_partner).start()

    load_sk.wait()
    for k in range(n):
        label = wrap(theirs + k - after)
        used = col_row < tab_s[me, 0, count + label]
        sk_out[k] = jnp.where(used, sk_v[label], 0.0)
    sk_copy = remote(sk_out, sk_b.at[1], sk_send, sk_recv, after_me)
    sk_copy.start()
    for k in range(n):
        label = wrap(half * n + k - after)
        kept = tab_s[me, 0, count + label]
        used = col_row < kept
        sk_b[0, k] = jnp.where(used, sk_v[label], 0.0)
        kept_s[0, k] = kept
        kept_s[1, k] = tab_s[before_me, 0, count + wrap(half * n + k - before)]
    gate_copy.wait()

    tile_rows = lax.broadcasted_iota(jnp.int32, (8, width), 0)
    ones = jnp.where(tile_rows < 2, 0.5, 0.0)
    st_own[0] = ones
    for kind in range(3):
        st_in[kind, 0] = ones
    acc[...] = jnp.zeros_like(acc)
    prev_w[...] = jnp.ones_like(prev_w)

    def travel_to(t):
        by = 2 - 4 * lax.rem(me + t, 2)
        last = t // (sweeps - 1)
        return last * odd_partner + (1 - last) * lax.rem(me + by + chain, chain)

    def near_of(t):
        return even_partner + lax.rem(t, 2) * (odd_partner - even_partner)

    def far_of(t):
        return odd_partner + lax.rem(t, 2) * (even_partner - odd_partner)

    def send_block(t, i):
        sweep = lax.rem(t, 2)
        trav_copy(t + 1, kk(i), travel_to(t)).start()
        if i == 0:

            @pl.when(t < sweeps - 1)
            def _():
                edge_copy(t + 1, 1 - sweep, OUT * sweep, kk(0), odd_partner).start()

        if i == n - 1:

            @pl.when(t < sweeps - 1)
            def _():
                edge_copy(
                    t + 1, sweep, OUT * (1 - sweep), kk(n - 1), even_partner
                ).start()

    def send_stats(t):
        stat_copy(t + 1, 0, near_of(t)).start()

        @pl.when(t < sweeps - 1)
        def _():
            stat_copy(t + 1, 1, travel_to(t)).start()
            stat_copy(t + 1, 2, far_of(t)).start()

    def fold_stats(t):
        now = st_own[t] + st_in[0, t]
        total, weight = now[0:1], now[1:2]
        acc[0:1] += 1.0 - weight / total
        acc[1:2] += jnp.log(total) - jnp.log(prev_w[0:1])
        return weight

    def one_sweep(t, carry):
        sweep = lax.rem(t, 2)
        is_left = half == sweep
        which = lax.rem(half + sweep, 2)
        left_in, right_in = which, 1 - which
        left_out = OUT * which
        right_out = OUT - left_out
        idle = (sweep == 1) & ((me == 0) | (me == chain - 1))
        first_edge = sweep

        def left_block(m):
            if m == 0:
                return n - half
            return n - 1 + half if m == n else jj(m) - 1

        def wait_block(m):
            if m == 0:

                @pl.when(t > 0)
                def _():
                    edge_copy(t, first_edge, OWN, 0, me).wait_recv()

            if m == n:
                edge_copy(t, 1 - first_edge, OWN, 0, me).wait_recv()
            if m < n:
                trav_copy(t, kk(m), me).wait_recv()

        def wait_stats():
            @pl.when(t > 0)
            def _():
                for kind in range(3):
                    stat_copy(t, kind, me).wait_recv()

            weight = fold_stats(t)
            other = st_in[1, t][1:2] + st_in[2, t][1:2]
            return jnp.where(is_left, weight, other)

        def stats(total, weight):
            st_own[t + 1] = jnp.where(tile_rows == 0, total, jnp.where(tile_rows == 1, weight, 0.0))

        @pl.when((t < 2) & jnp.logical_not(is_left))
        def _():
            sk_copy.wait_recv()

        @pl.when(idle)
        def _():
            for m in range(n + 1):
                wait_block(m)
            left_w = wait_stats()
            scale = 1.0 / jnp.sqrt(left_w)
            for i in range(n):
                k = kk(i)
                below = n - 2 * half if i == 0 else n - 2 + 2 * half if i == n - 1 else k - 1
                big[left_out, t + 1, k, 0] = scale * big[left_in, t, k, 0]
                big[left_out, t + 1, k, 1] = scale * big[left_in, t, below, 1]
                big[right_out, t + 1, k, 0] = big[right_in, t, k, 0]
                big[right_out, t + 1, k, 1] = big[right_in, t, k + 1, 1]
                send_block(t, i)
            stats(0.5, 0.5)
            send_stats(t)
            prev_w[...] = jnp.ones_like(prev_w)

        @pl.when(jnp.logical_not(idle))
        def _():
            g = [gate_v[which, 0:1, i : i + 1] for i in range(6)]
            tot[...] = jnp.zeros_like(tot)
            wgt[...] = jnp.zeros_like(wgt)

            for m in range(n + 1):
                wait_block(m)
                j = jj(m)
                jl = left_block(m)
                lx = [big[left_in, t, jl, p] for p in range(2)]
                rx = [big[right_in, t, j, p] for p in range(2)]
                s01 = mm(lx[0], rx[1])
                s10 = mm(lx[1], rx[0])
                mat[j, :width, width:] = g[2] * s01 + g[3] * s10
                mat[j + 1, width:, :width] = g[4] * s01 + g[5] * s10
                if m == 0:
                    last = (lx, rx)
                    continue
                k = kk(m - 1)
                plx, prx = last
                last = (lx, rx)
                l0 = jnp.where(odd, plx[0], lx[0])
                l1 = jnp.where(odd, lx[1], plx[1])
                r0 = jnp.where(odd, rx[0], prx[0])
                r1 = jnp.where(odd, prx[1], rx[1])
                mat[k + 1, :width, :width] = g[0] * mm(l0, r0)
                mat[k + 1, width:, width:] = g[1] * mm(l1, r1)
                mk = mat[k + 1]
                sq = jnp.sum(mk * mk, axis=0, keepdims=True)
                tot[0:1, :] += sq[:, :width] + sq[:, width:]
                s = mm(mk, sk_b[which, k])
                smp[k] = s
                w_ref[k] = mm(s, s, 0, 0)

            left_w = wait_stats()
            for k in range(n):
                s = smp[k]
                used = col_row < kept_s[which, k]
                ds = jnp.sum(jnp.sum(s * s, axis=0, keepdims=True), axis=1, keepdims=True)
                kf = kept_s[which, k].astype(f32)
                ridge = 0.001 * ds / kf + 1e-06 * left_w
                add = ridge + jnp.where(used, 0.0, 1.0)
                w_ref[k] = w_ref[k] + jnp.where(eye, add, 0.0)
            inverse_factors(w_ref, z_ref, n, width)

            for i in range(n):
                k = kk(i)
                basis = mm(smp[k], z_ref[k], 1, 1)
                red = mm(basis, mat[k + 1], 0, 0)
                sq = jnp.sum(red * red, axis=0, keepdims=True)
                wgt[0:1, :] += sq[:, :width] + sq[:, width:]
                for p in range(2):
                    big[left_out, t + 1, k, p] = basis[p * width : (p + 1) * width]
                    big[right_out, t + 1, k, p] = red[:, p * width : (p + 1) * width]
                send_block(t, i)
            stats(
                jnp.sum(tot[0:1, :], axis=1, keepdims=True),
                jnp.sum(wgt[0:1, :], axis=1, keepdims=True),
            )
            send_stats(t)
            prev_w[...] = jnp.broadcast_to(left_w, prev_w.shape)

        return carry

    lax.fori_loop(0, sweeps, one_sweep, 0)

    stat_copy(sweeps, 0, me).wait_recv()
    weight = fold_stats(sweeps)
    all_v[me] = 0.5 * acc[...]

    def sum_copy(off):
        return remote(
            all_v.at[me], all_v.at[me], sum_send.at[off], sum_recv.at[off],
            lax.rem(me + off, chain),
        )

    def begin_sum(off, carry):
        sum_copy(off).start()
        return carry

    def finish_sum(off, carry):
        sum_copy(off).wait()
        return carry

    lax.fori_loop(1, chain, begin_sum, 0)
    scale = jnp.where(odd, 1.0, 1.0 / jnp.sqrt(weight))
    for k in range(n):
        trav_copy(sweeps, k, me).wait_recv()
    for p in range(2):
        for l in range(count):
            index = wrap(l + before + half * p + half * n)
            far = (index >= n).astype(jnp.int32)
            out[p * count + l] = big[far, sweeps, index - n * far, p] * scale
    lax.fori_loop(1, chain, finish_sum, 0)
    sums[...] = jnp.sum(all_v[...], axis=0)

    sk_copy.wait_send()
    edge_copy(0, 1, OWN, 0, me).wait_send()

    def drain(t, carry):
        for k in range(n):
            trav_copy(t, k, me).wait_send()

        @pl.when((t > 0) & (t < sweeps))
        def _():
            for kind in range(2):
                edge_copy(t, kind, OWN, 0, me).wait_send()
            for kind in range(1, 3):
                stat_copy(t, kind, me).wait_send()

        @pl.when(t > 0)
        def _():
            stat_copy(t, 0, me).wait_send()

        return carry

    lax.fori_loop(0, sweeps + 1, drain, 0)


def run_chain(n, width, chain, table, gate_tile, sites, sketches):
    f32, i32 = jnp.float32, jnp.int32
    count, slots = 2 * n, 2 * STEPS + 1
    vmem = pl.BlockSpec(memory_space=pltpu.VMEM)
    anywhere = pl.BlockSpec(memory_space=pl.ANY)
    dma = pltpu.SemaphoreType.DMA
    return pl.pallas_call(
        functools.partial(chain_kernel, n, width, chain),
        out_shape=(
            jax.ShapeDtypeStruct((2 * count, width, width), f32),
            jax.ShapeDtypeStruct((8, width), f32),
        ),
        in_specs=[vmem, vmem, anywhere, anywhere],
        out_specs=(vmem, vmem),
        scratch_shapes=[
            pltpu.VMEM((2 * count, width, width), f32),
            pltpu.VMEM((count, 2 * width, width), f32),
            pltpu.VMEM((chain, 1, width), i32),
            pltpu.SMEM((chain, 1, width), i32),
            pltpu.VMEM((2, 8, width), f32),
            pltpu.SMEM((2, n), i32),
            pltpu.VMEM((n, 2 * width, width), f32),
            pltpu.VMEM((2, n, 2 * width, width), f32),
            pltpu.VMEM((3, slots, n + 1, 2, width, width), f32),
            pltpu.VMEM((slots, 8, width), f32),
            pltpu.VMEM((3, slots, 8, width), f32),
            pltpu.VMEM((chain, 8, width), f32),
            pltpu.VMEM((8, width), f32),
            pltpu.VMEM((8, width), f32),
            pltpu.VMEM((n + 2, 2 * width, 2 * width), f32),
            pltpu.VMEM((n, 2 * width, width), f32),
            pltpu.VMEM((n, width, width), f32),
            pltpu.VMEM((n, width, width), f32),
            pltpu.VMEM((8, width), f32),
            pltpu.VMEM((8, width), f32),
            dma((3,)),
            dma((chain,)),
            dma((chain,)),
            dma((2,)),
            dma,
            dma,
            dma((slots, n)),
            dma((slots, n)),
            dma((slots, 2)),
            dma((slots, 2)),
            dma((slots, 3)),
            dma((slots, 3)),
            dma((chain,)),
            dma((chain,)),
        ],
        compiler_params=pltpu.CompilerParams(
            collective_id=1, has_side_effects=True, vmem_limit_bytes=56 * 1024 * 1024
        ),
    )(table, gate_tile, sites, sketches)


def body(sites, sector_sizes, charge_steps, kept_counts, gates, sketches):
    chain = lax.axis_size("site")
    count, width = sites.shape[2], sites.shape[-1]
    n = count // 2
    table = jnp.concatenate([sector_sizes, kept_counts, charge_steps[:, None]], axis=1)
    table = jnp.pad(table, ((0, 0), (0, width - table.shape[1])))
    gate_tile = jnp.pad(gates, ((0, 7), (0, width - gates.shape[1])))
    out, sums = run_chain(
        n, width, chain, table, gate_tile,
        sites.reshape(2 * count, width, width), sketches.reshape(count, 2 * width, width),
    )
    return out.reshape(sites.shape), sums[:2, 0]


def solution(mesh):
    placed = (
        P("site", None, None, None, None),
        P("site", None),
        P("site"),
        P("site", None),
        P("site", None),
        P("site", None, None, None),
    )
    return jax.shard_map(
        body,
        mesh=mesh,
        in_specs=placed,
        out_specs=(P("site", None, None, None, None), P()),
        check_vma=False,
    )
```

```python
import functools

import jax
import jax.numpy as jnp
from jax import lax
from jax.experimental import pallas as pl
from jax.experimental.pallas import tpu as pltpu
from jax.sharding import PartitionSpec as P

STEPS = 4
HI = lax.Precision.HIGHEST
MESH = pl.DeviceIdType.MESH
OWN, IN, OUT = 0, 1, 2


def mm(a, b, ca=1, cb=0):
    return lax.dot_general(
        a, b, (((ca,), (cb,)), ((), ())), precision=HI, preferred_element_type=jnp.float32
    )


def inverse_factors(w_ref, z_ref, n, width):
    strip = 32
    lanes = lax.broadcasted_iota(jnp.int32, (1, 8, width), 2)
    subs = lax.broadcasted_iota(jnp.int32, (1, 8, width), 1)
    for b in range(width // strip):
        r0 = b * strip
        groups = strip // 8
        ps = [w_ref[:, r0 + 8 * g : r0 + 8 * g + 8, :] for g in range(groups)]
        if b == 0:
            zs = [
                jnp.broadcast_to((lanes == subs + 8 * g).astype(jnp.float32), ps[0].shape)
                for g in range(groups)
            ]
        else:
            zs = [z_ref[:, r0 + 8 * g : r0 + 8 * g + 8, :] for g in range(groups)]
        for q in range(groups):
            vs = [
                [
                    jnp.broadcast_to(
                        ps[g][:, :, r0 + 8 * q + t : r0 + 8 * q + t + 1], ps[g].shape
                    )
                    if g >= q
                    else None
                    for g in range(groups)
                ]
                for t in range(8)
            ]
            root = jnp.zeros_like(ps[q])
            for t in range(8):
                piv = vs[t][q][:, t : t + 1, :]
                inv = lax.rsqrt(piv)
                inv = inv * (1.5 - 0.5 * piv * inv * inv)
                inv2 = inv * inv
                root = jnp.where(subs == t, inv, root)
                below = jnp.where(subs > t, vs[t][q], 0.0)

                def eliminate(rows):
                    scaled = rows[q][:, t : t + 1, :] * inv2
                    out = list(rows)
                    if t < 7:
                        out[q] = rows[q] - below * scaled
                    for g in range(q + 1, groups):
                        out[g] = rows[g] - vs[t][g] * scaled
                    return out

                ps = eliminate(ps)
                zs = eliminate(zs)
                for t2 in range(t + 1, 8):
                    vs[t2] = eliminate(vs[t2])
            ps[q] = ps[q] * root
            zs[q] = zs[q] * root
        for g in range(groups):
            z_ref[:, r0 + 8 * g : r0 + 8 * g + 8, :] = zs[g]
            w_ref[:, r0 + 8 * g : r0 + 8 * g + 8, :] = ps[g]
        r1 = r0 + strip
        if r1 < width:
            rest = width - r1

            def trail(k, carry, r0=r0, r1=r1, rest=rest, b=b):
                pk = w_ref[k, r0:r1, :]
                zk = z_ref[k, r0:r1, :]
                both = mm(pk, jnp.concatenate([pk, zk], axis=1), 0, 0)[r1:]
                w_ref[k, r1:, :] = w_ref[k, r1:, :] - both[:, :width]
                if b == 0:
                    ri = lax.broadcasted_iota(jnp.int32, (rest, width), 0) + r1
                    ci = lax.broadcasted_iota(jnp.int32, (rest, width), 1)
                    old = (ri == ci).astype(jnp.float32)
                else:
                    old = z_ref[k, r1:, :]
                z_ref[k, r1:, :] = old - both[:, width:]
                return carry

            lax.fori_loop(0, n, trail, 0, unroll=True)


def chain_kernel(
    n, width, chain,
    table, gate_tile, sites, sketches,
    out, sums,
    sites_v, sk_v, tab_v, tab_s, gate_v, kept_s, sk_out, sk_b,
    big, st_own, st_in, all_v, acc, prev_w, mat, smp, w_ref, z_ref, tot, wgt,
    load_sem, bar_send, bar_recv, gate_send, gate_recv, sk_send, sk_recv, tr_send, tr_recv,
    own_send, own_recv,
    ed_send, ed_recv, st_send, st_recv, sum_send, sum_recv,
):
    f32 = jnp.float32
    count = 2 * n
    sweeps = 2 * STEPS
    pos = lax.axis_index("site")

    def place(q):
        return q + lax.rem(q, 2) - lax.rem(lax.div(q, 2), 2) if chain % 4 == 0 else q

    me = place(pos)
    bit = lax.rem(pos, 2)
    home = lax.rem(me, 2)
    moved = lax.rem(bit + home, 2)
    is_moved = moved == 1
    after_pos = lax.rem(pos + 1, chain)
    before_pos = lax.rem(pos + chain - 1, chain)
    before_me = lax.rem(me + chain - 1, chain)
    keeps_next = place(after_pos) == pos

    def even_partner(q):
        return q + 1 - 2 * lax.rem(q, 2)

    def odd_partner(q):
        return lax.rem(q - 1 + 2 * lax.rem(q, 2) + chain, chain)

    load_sites = pltpu.make_async_copy(sites, sites_v, load_sem.at[0])
    load_sk = pltpu.make_async_copy(sketches, sk_v, load_sem.at[1])
    load_sites.start()
    load_sk.start()

    barrier = pltpu.get_barrier_semaphore()

    def greet(off, carry):
        pl.semaphore_signal(
            barrier, inc=1, device_id=(lax.rem(pos + off, chain),), device_id_type=MESH
        )
        return carry

    lax.fori_loop(1, chain, greet, 0)
    pl.semaphore_wait(barrier, chain - 1)

    def remote(src, dst, send, recv, to):
        return pltpu.make_async_remote_copy(
            src_ref=src, dst_ref=dst, send_sem=send, recv_sem=recv,
            device_id=(to,), device_id_type=MESH,
        )

    def table_copy(off):
        return remote(
            table, tab_v.at[pos], bar_send.at[off], bar_recv.at[off], lax.rem(pos + off, chain)
        )

    def begin_table(off, carry):
        table_copy(off).start()
        return carry

    def finish_table(off, carry):
        table_copy(off).wait()
        return carry

    lax.fori_loop(1, chain, begin_table, 0)

    def gate_copy(i, to):
        return remote(gate_tile, gate_v.at[i], gate_send.at[i], gate_recv.at[i], to)

    gate_copy(1, after_pos).start()

    @pl.when(is_moved)
    def _():
        gate_copy(2, me).start()

    @pl.when(jnp.logical_not(keeps_next))
    def _():
        gate_copy(3, place(after_pos)).start()

    tab_v[pos] = table[...]
    gate_v[0] = gate_tile[...]

    @pl.when(jnp.logical_not(is_moved))
    def _():
        gate_v[2] = gate_tile[...]

    @pl.when(keeps_next)
    def _():
        gate_v[3] = gate_tile[...]

    lax.fori_loop(1, chain, finish_table, 0)
    to_scalar = pltpu.make_async_copy(tab_v, tab_s, load_sem.at[2])
    to_scalar.start()
    to_scalar.wait()

    def charge_before(site):
        def add_step(d, total):
            return total + jnp.where(d < site, tab_s[d, 0, 2 * count], 0)

        return lax.rem(lax.fori_loop(0, chain, add_step, jnp.int32(0)), count)

    before = charge_before(pos)
    step = tab_s[pos, 0, 2 * count]
    after = before + step
    me_before = charge_before(me)
    me_after = me_before + tab_s[me, 0, 2 * count]

    def wrap(x):
        return lax.rem(x + 2 * count, count)

    row_ids = lax.broadcasted_iota(jnp.int32, (width, width), 0)
    col_ids = lax.broadcasted_iota(jnp.int32, (width, width), 1)
    col_row = lax.broadcasted_iota(jnp.int32, (1, width), 1)
    eye = row_ids == col_ids

    load_sites.wait()

    def block(charge, p):
        label = wrap(charge - before - bit * p)
        target = wrap(label + p - step)
        rows = tab_s[pos, 0, label]
        cols = tab_s[after_pos, 0, target]
        keep = (row_ids < rows) & (col_ids < cols)
        return jnp.where(keep, sites_v[p * count + label], 0.0)

    theirs = (1 - bit) * n

    def trav_copy(t, k, to):
        return remote(
            big.at[OUT, t, k], big.at[IN, t, k], tr_send.at[t, k], tr_recv.at[t, k], to
        )

    def own_copy(k):
        return remote(
            big.at[OWN, sweeps + 1, k], big.at[OWN, 1, k], own_send.at[k], own_recv.at[k], me
        )

    def edge_copy(t, kind, src, slot, k, to):
        return remote(
            big.at[src, slot, k], big.at[kind, t, n], ed_send.at[t, kind], ed_recv.at[t, kind], to
        )

    def stat_copy(t, kind, slot, to):
        return remote(
            st_own.at[slot], st_in.at[kind, t], st_send.at[t, kind], st_recv.at[t, kind], to
        )

    def own_stat_copy():
        return remote(
            st_own.at[sweeps + 1], st_own.at[1], own_send.at[n], own_recv.at[n], me
        )

    for i in range(n):
        k = n - 1 - i + bit * (2 * i - n + 1)
        for p in range(2):
            big[OUT, 0, k, p] = block(theirs + k, p)
        trav_copy(0, k, even_partner(pos)).start()
    for i in range(n):
        k = n - 1 - i
        for p in range(2):
            big[OWN, 0, k, p] = block(bit * n + k, p)
    last_k = n - 1 - bit * (n - 1)
    for p in range(2):
        big[OWN, 0, n, p] = big[OUT, 0, last_k, p]
    edge_copy(0, 1, OWN, 0, last_k, even_partner(pos)).start()

    load_sk.wait()
    for k in range(n):
        label = wrap(theirs + k - after)
        used = col_row < tab_s[pos, 0, count + label]
        sk_out[k] = jnp.where(used, sk_v[label], 0.0)

    def sk_copy(i, src, to):
        return remote(src, sk_b.at[i], sk_send.at[i], sk_recv.at[i], to)

    @pl.when(bit == 0)
    def _():
        sk_copy(1, sk_out, after_pos).start()

    for k in range(n):
        label = wrap(bit * n + k - after)
        kept = tab_s[pos, 0, count + label]
        used = col_row < kept
        sk_b[0, k] = jnp.where(used, sk_v[label], 0.0)
        kept_s[0, k] = kept
        kept_s[1, k] = tab_s[before_pos, 0, count + wrap(bit * n + k - before)]
        kept_s[2, k] = tab_s[me, 0, count + wrap(home * n + k - me_after)]
        kept_s[3, k] = tab_s[before_me, 0, count + wrap(home * n + k - me_before)]

    @pl.when(is_moved)
    def _():
        sk_copy(2, sk_b.at[0], me).start()

    @pl.when(jnp.logical_not(keeps_next))
    def _():
        sk_copy(3, sk_out, place(after_pos)).start()

    @pl.when(jnp.logical_not(is_moved))
    def _():
        for k in range(n):
            sk_b[2, k] = sk_b[0, k]

    @pl.when(keeps_next)
    def _():
        for k in range(n):
            sk_b[3, k] = sk_out[k]

    gate_copy(1, after_pos).wait()

    @pl.when(is_moved)
    def _():
        gate_copy(2, me).wait()

    @pl.when(jnp.logical_not(keeps_next))
    def _():
        gate_copy(3, place(after_pos)).wait()

    tile_rows = lax.broadcasted_iota(jnp.int32, (8, width), 0)
    ones = jnp.where(tile_rows < 2, 0.5, 0.0)
    st_own[0] = ones
    for kind in range(3):
        st_in[kind, 0] = ones
    acc[...] = jnp.zeros_like(acc)
    prev_w[...] = jnp.ones_like(prev_w)

    def fold_stats(t):
        now = st_own[t] + st_in[0, t]
        total, weight = now[0:1], now[1:2]
        acc[0:1] += 1.0 - weight / total
        acc[1:2] += jnp.log(total) - jnp.log(prev_w[0:1])
        return weight

    def one_sweep(t, carry):
        sweep = lax.rem(t, 2)
        first = 1 - lax.div(t + sweeps - 1, sweeps)
        last = lax.div(t, sweeps - 1)
        q = first * pos + (1 - first) * me
        half = lax.rem(q, 2)
        odd = half == 1
        is_left = half == sweep
        first_moved = (t == 0) & is_moved
        second_moved = (t == 1) & is_moved

        def kk(i):
            return i + half * (n - 1 - 2 * i)

        def jj(m):
            return m + half * (n - 2 * m)

        which = lax.rem(half + sweep, 2)
        left_in, right_in = which, 1 - which
        own_kind = OUT * last * moved
        trav_kind = OUT - own_kind
        own_slot = t + 1 + first * moved * sweeps
        left_out = own_kind + which * (trav_kind - own_kind)
        right_out = OUT - left_out
        left_slot = own_slot + which * (t + 1 - own_slot)
        right_slot = own_slot + t + 1 - left_slot
        table_row = which + 2 * (1 - first)
        idle = (sweep == 1) & ((q == 0) | (q == chain - 1))
        first_edge = sweep

        def left_block(m):
            if m == 0:
                return n - half
            return n - 1 + half if m == n else jj(m) - 1

        ends = last * (moved * me + (1 - moved) * odd_partner(q))
        by = 2 - 4 * lax.rem(q + t, 2)
        travel = ends + (1 - last) * place(lax.rem(q + by + chain, chain))
        even_to = place(even_partner(q))
        odd_to = place(odd_partner(q))

        def send_block(i):
            k = kk(i)
            trav_copy(t + 1, k, travel).start()

            @pl.when(first_moved)
            def _():
                own_copy(k).start()

            if i == 0:

                @pl.when(first_moved)
                def _():
                    for p in range(2):
                        big[IN, 1, n, p] = big[OWN, sweeps + 1, k, p]

                @pl.when((t < sweeps - 1) & jnp.logical_not(first_moved))
                def _():
                    edge_copy(t + 1, 1 - sweep, OUT * sweep, t + 1, k, odd_to).start()

            if i == n - 1:

                @pl.when(t < sweeps - 1)
                def _():
                    edge_copy(t + 1, sweep, OUT * (1 - sweep), t + 1, k, even_to).start()

        def send_stats():
            near = even_to + sweep * (odd_to - even_to)
            far = odd_to + even_to - near
            stat_copy(t + 1, 0, own_slot, near).start()

            @pl.when(t < sweeps - 1)
            def _():
                stat_copy(t + 1, 1, own_slot, travel).start()

            @pl.when((t < sweeps - 1) & jnp.logical_not(first_moved))
            def _():
                stat_copy(t + 1, 2, own_slot, far).start()

            @pl.when(first_moved)
            def _():
                own_stat_copy().start()
                st_in[2, 1] = st_own[sweeps + 1]

        def wait_block(m):
            if m == 0:

                @pl.when((t > 0) & jnp.logical_not(second_moved))
                def _():
                    edge_copy(t, first_edge, OWN, 0, 0, even_to).wait_recv()

            if m == n:
                edge_copy(t, 1 - first_edge, OWN, 0, 0, even_to).wait_recv()
            if m < n:
                trav_copy(t, kk(m), even_to).wait_recv()

                @pl.when(second_moved)
                def _():
                    own_copy(kk(m)).wait_recv()

        def wait_stats():
            @pl.when(t > 0)
            def _():
                for kind in range(2):
                    stat_copy(t, kind, 0, even_to).wait_recv()

            @pl.when((t > 0) & jnp.logical_not(second_moved))
            def _():
                stat_copy(t, 2, 0, even_to).wait_recv()

            @pl.when(second_moved)
            def _():
                own_stat_copy().wait_recv()

            weight = fold_stats(t)
            other = st_in[1, t][1:2] + st_in[2, t][1:2]
            return jnp.where(is_left, weight, other)

        def stats(total, weight):
            st_own[own_slot] = jnp.where(tile_rows == 0, total, jnp.where(tile_rows == 1, weight, 0.0))

        early = (t > 0) & (t < 3)

        @pl.when((t == 0) & (half == 1))
        def _():
            sk_copy(1, sk_out, even_to).wait_recv()

        @pl.when(early & is_left & is_moved)
        def _():
            sk_copy(2, sk_out, even_to).wait_recv()

        @pl.when(early & jnp.logical_not(is_left) & jnp.logical_not(keeps_next))
        def _():
            sk_copy(3, sk_out, even_to).wait_recv()

        @pl.when(idle)
        def _():
            for m in range(n + 1):
                wait_block(m)
            left_w = wait_stats()
            scale = 1.0 / jnp.sqrt(left_w)
            for i in range(n):
                k = kk(i)
                below = n - 2 * half if i == 0 else n - 2 + 2 * half if i == n - 1 else k - 1
                big[left_out, left_slot, k, 0] = scale * big[left_in, t, k, 0]
                big[left_out, left_slot, k, 1] = scale * big[left_in, t, below, 1]
                big[right_out, right_slot, k, 0] = big[right_in, t, k, 0]
                big[right_out, right_slot, k, 1] = big[right_in, t, k + 1, 1]
                send_block(i)
            stats(0.5, 0.5)
            send_stats()
            prev_w[...] = jnp.ones_like(prev_w)

        @pl.when(jnp.logical_not(idle))
        def _():
            g = [gate_v[table_row, 0:1, i : i + 1] for i in range(6)]
            tot[...] = jnp.zeros_like(tot)
            wgt[...] = jnp.zeros_like(wgt)

            for m in range(n + 1):
                wait_block(m)
                j = jj(m)
                jl = left_block(m)
                lx = [big[left_in, t, jl, p] for p in range(2)]
                rx = [big[right_in, t, j, p] for p in range(2)]
                s01 = mm(lx[0], rx[1])
                s10 = mm(lx[1], rx[0])
                mat[j, :width, width:] = g[2] * s01 + g[3] * s10
                mat[j + 1, width:, :width] = g[4] * s01 + g[5] * s10
                if m == 0:
                    last = (lx, rx)
                    continue
                k = kk(m - 1)
                plx, prx = last
                last = (lx, rx)
                l0 = jnp.where(odd, plx[0], lx[0])
                l1 = jnp.where(odd, lx[1], plx[1])
                r0 = jnp.where(odd, rx[0], prx[0])
                r1 = jnp.where(odd, prx[1], rx[1])
                mat[k + 1, :width, :width] = g[0] * mm(l0, r0)
                mat[k + 1, width:, width:] = g[1] * mm(l1, r1)
                mk = mat[k + 1]
                sq = jnp.sum(mk * mk, axis=0, keepdims=True)
                tot[0:1, :] += sq[:, :width] + sq[:, width:]
                s = mm(mk, sk_b[table_row, k])
                smp[k] = s
                w_ref[k] = mm(s, s, 0, 0)

            left_w = wait_stats()
            for k in range(n):
                s = smp[k]
                used = col_row < kept_s[table_row, k]
                ds = jnp.sum(jnp.sum(s * s, axis=0, keepdims=True), axis=1, keepdims=True)
                kf = kept_s[table_row, k].astype(f32)
                ridge = 0.001 * ds / kf + 1e-06 * left_w
                add = ridge + jnp.where(used, 0.0, 1.0)
                w_ref[k] = w_ref[k] + jnp.where(eye, add, 0.0)
            inverse_factors(w_ref, z_ref, n, width)

            for i in range(n):
                k = kk(i)
                basis = mm(smp[k], z_ref[k], 1, 1)
                red = mm(basis, mat[k + 1], 0, 0)
                sq = jnp.sum(red * red, axis=0, keepdims=True)
                wgt[0:1, :] += sq[:, :width] + sq[:, width:]
                for p in range(2):
                    big[left_out, left_slot, k, p] = basis[p * width : (p + 1) * width]
                    big[right_out, right_slot, k, p] = red[:, p * width : (p + 1) * width]
                send_block(i)
            stats(
                jnp.sum(tot[0:1, :], axis=1, keepdims=True),
                jnp.sum(wgt[0:1, :], axis=1, keepdims=True),
            )
            send_stats()
            prev_w[...] = jnp.broadcast_to(left_w, prev_w.shape)

        return carry

    lax.fori_loop(0, sweeps, one_sweep, 0)

    stat_copy(sweeps, 0, 0, after_pos).wait_recv()
    weight = fold_stats(sweeps)
    all_v[pos] = 0.5 * acc[...]

    def sum_copy(off):
        return remote(
            all_v.at[pos], all_v.at[pos], sum_send.at[off], sum_recv.at[off],
            lax.rem(pos + off, chain),
        )

    def begin_sum(off, carry):
        sum_copy(off).start()
        return carry

    def finish_sum(off, carry):
        sum_copy(off).wait()
        return carry

    lax.fori_loop(1, chain, begin_sum, 0)
    scale = jnp.where(bit == 1, 1.0, 1.0 / jnp.sqrt(weight))
    for k in range(n):
        trav_copy(sweeps, k, after_pos).wait_recv()
    for p in range(2):
        for l in range(count):
            index = wrap(l + before + bit * p + home * n)
            far = (index >= n).astype(jnp.int32)
            out[p * count + l] = big[far, sweeps, index - n * far, p] * scale
    lax.fori_loop(1, chain, finish_sum, 0)
    sums[...] = jnp.sum(all_v[...], axis=0)

    @pl.when(bit == 0)
    def _():
        sk_copy(1, sk_out, after_pos).wait_send()

    @pl.when(jnp.logical_not(keeps_next))
    def _():
        sk_copy(3, sk_out, after_pos).wait_send()

    @pl.when(is_moved)
    def _():
        sk_copy(2, sk_out, after_pos).wait_send()
        own_stat_copy().wait_send()
        for k in range(n):
            own_copy(k).wait_send()

    edge_copy(0, 1, OWN, 0, 0, after_pos).wait_send()

    def drain(t, carry):
        for k in range(n):
            trav_copy(t, k, after_pos).wait_send()

        inner = (t > 0) & (t < sweeps)
        here = (t == 1) & is_moved

        @pl.when(inner)
        def _():
            edge_copy(t, 0, OWN, 0, 0, after_pos).wait_send()
            stat_copy(t, 1, 0, after_pos).wait_send()

        @pl.when(inner & jnp.logical_not(here))
        def _():
            edge_copy(t, 1, OWN, 0, 0, after_pos).wait_send()
            stat_copy(t, 2, 0, after_pos).wait_send()

        @pl.when(t > 0)
        def _():
            stat_copy(t, 0, 0, after_pos).wait_send()

        return carry

    lax.fori_loop(0, sweeps + 1, drain, 0)


def run_chain(n, width, chain, table, gate_tile, sites, sketches):
    f32, i32 = jnp.float32, jnp.int32
    count, slots = 2 * n, 2 * STEPS + 1
    vmem = pl.BlockSpec(memory_space=pltpu.VMEM)
    anywhere = pl.BlockSpec(memory_space=pl.ANY)
    dma = pltpu.SemaphoreType.DMA
    return pl.pallas_call(
        functools.partial(chain_kernel, n, width, chain),
        out_shape=(
            jax.ShapeDtypeStruct((2 * count, width, width), f32),
            jax.ShapeDtypeStruct((8, width), f32),
        ),
        in_specs=[vmem, vmem, anywhere, anywhere],
        out_specs=(vmem, vmem),
        scratch_shapes=[
            pltpu.VMEM((2 * count, width, width), f32),
            pltpu.VMEM((count, 2 * width, width), f32),
            pltpu.VMEM((chain, 1, width), i32),
            pltpu.SMEM((chain, 1, width), i32),
            pltpu.VMEM((4, 8, width), f32),
            pltpu.SMEM((4, n), i32),
            pltpu.VMEM((n, 2 * width, width), f32),
            pltpu.VMEM((4, n, 2 * width, width), f32),
            pltpu.VMEM((3, slots + 1, n + 1, 2, width, width), f32),
            pltpu.VMEM((slots + 1, 8, width), f32),
            pltpu.VMEM((3, slots, 8, width), f32),
            pltpu.VMEM((chain, 8, width), f32),
            pltpu.VMEM((8, width), f32),
            pltpu.VMEM((8, width), f32),
            pltpu.VMEM((n + 2, 2 * width, 2 * width), f32),
            pltpu.VMEM((n, 2 * width, width), f32),
            pltpu.VMEM((n, width, width), f32),
            pltpu.VMEM((n, width, width), f32),
            pltpu.VMEM((8, width), f32),
            pltpu.VMEM((8, width), f32),
            dma((3,)),
            dma((chain,)),
            dma((chain,)),
            dma((4,)),
            dma((4,)),
            dma((4,)),
            dma((4,)),
            dma((slots, n)),
            dma((slots, n)),
            dma((n + 1,)),
            dma((n + 1,)),
            dma((slots, 2)),
            dma((slots, 2)),
            dma((slots, 3)),
            dma((slots, 3)),
            dma((chain,)),
            dma((chain,)),
        ],
        compiler_params=pltpu.CompilerParams(
            collective_id=1, has_side_effects=True, vmem_limit_bytes=56 * 1024 * 1024
        ),
    )(table, gate_tile, sites, sketches)


def body(sites, sector_sizes, charge_steps, kept_counts, gates, sketches):
    chain = lax.axis_size("site")
    count, width = sites.shape[2], sites.shape[-1]
    n = count // 2
    table = jnp.concatenate([sector_sizes, kept_counts, charge_steps[:, None]], axis=1)
    table = jnp.pad(table, ((0, 0), (0, width - table.shape[1])))
    gate_tile = jnp.pad(gates, ((0, 7), (0, width - gates.shape[1])))
    out, sums = run_chain(
        n, width, chain, table, gate_tile,
        sites.reshape(2 * count, width, width), sketches.reshape(count, 2 * width, width),
    )
    return out.reshape(sites.shape), sums[:2, 0]


def solution(mesh):
    placed = (
        P("site", None, None, None, None),
        P("site", None),
        P("site"),
        P("site", None),
        P("site", None),
        P("site", None, None, None),
    )
    return jax.shard_map(
        body,
        mesh=mesh,
        in_specs=placed,
        out_specs=(P("site", None, None, None, None), P()),
        check_vma=False,
    )
```

```python
import functools

import jax
import jax.numpy as jnp
from jax import lax
from jax.experimental import pallas as pl
from jax.experimental.pallas import tpu as pltpu
from jax.sharding import PartitionSpec as P

STEPS = 4
HI = lax.Precision.HIGHEST
MESH = pl.DeviceIdType.MESH
OWN, IN, OUT = 0, 1, 2
TAKE, GIVE = (2, 2, 3), (2, 2)


def groups_of(total, sizes):
    out, at = [], 0
    while at < total:
        size = sizes[min(len(out), len(sizes) - 1)]
        out.append(range(at, min(at + size, total)))
        at += size
    return out


def mm(a, b, ca=1, cb=0):
    return lax.dot_general(
        a, b, (((ca,), (cb,)), ((), ())), precision=HI, preferred_element_type=jnp.float32
    )


def split3(a):
    bf16, f32 = jnp.bfloat16, jnp.float32
    a1 = a.astype(bf16)
    rest = a - a1.astype(f32)
    a2 = rest.astype(bf16)
    return a1, a2, (rest - a2.astype(f32)).astype(bf16)


def rank_update(pk, zk, width):
    b1, b2, b3 = split3(jnp.concatenate([pk, zk], axis=1))
    a1, a2, a3 = (b[:, :width] for b in (b1, b2, b3))
    return lax.dot_general(
        jnp.concatenate([a3, a1, a2, a2, a1, a1], axis=0),
        jnp.concatenate([b1, b3, b2, b1, b2, b1], axis=0),
        (((0,), (0,)), ((), ())), preferred_element_type=jnp.float32,
    )


def inverse_factors(w_ref, z_ref, n, width):
    strip, ahead = 32, 4
    lanes = lax.broadcasted_iota(jnp.int32, (1, 8, width), 2)
    subs = lax.broadcasted_iota(jnp.int32, (1, 8, width), 1)
    for b in range(width // strip):
        r0 = b * strip
        groups = strip // 8
        ps = [w_ref[:, r0 + 8 * g : r0 + 8 * g + 8, :] for g in range(groups)]
        if b == 0:
            zs = [
                jnp.broadcast_to((lanes == subs + 8 * g).astype(jnp.float32), ps[0].shape)
                for g in range(groups)
            ]
        else:
            zs = [z_ref[:, r0 + 8 * g : r0 + 8 * g + 8, :] for g in range(groups)]
        for q in range(groups):
            root = jnp.zeros_like(ps[q])
            for h in range(0, 8, ahead):
                c0 = r0 + 8 * q + h
                vs = [
                    [
                        jnp.broadcast_to(ps[g][:, :, c0 + t : c0 + t + 1], ps[g].shape)
                        if g >= q
                        else None
                        for g in range(groups)
                    ]
                    for t in range(ahead)
                ]
                for t in range(ahead):
                    row = h + t
                    piv = vs[t][q][:, row : row + 1, :]
                    inv = lax.rsqrt(piv)
                    inv = inv * (1.5 - 0.5 * piv * inv * inv)
                    inv2 = inv * inv
                    root = jnp.where(subs == row, inv, root)
                    below = jnp.where(subs > row, vs[t][q], 0.0)

                    def eliminate(rows):
                        scaled = rows[q][:, row : row + 1, :] * inv2
                        out = list(rows)
                        if row < 7:
                            out[q] = rows[q] - below * scaled
                        for g in range(q + 1, groups):
                            out[g] = rows[g] - vs[t][g] * scaled
                        return out

                    ps = eliminate(ps)
                    zs = eliminate(zs)
                    for t2 in range(t + 1, ahead):
                        vs[t2] = eliminate(vs[t2])
            ps[q] = ps[q] * root
            zs[q] = zs[q] * root
        for g in range(groups):
            z_ref[:, r0 + 8 * g : r0 + 8 * g + 8, :] = zs[g]
            w_ref[:, r0 + 8 * g : r0 + 8 * g + 8, :] = ps[g]
        r1 = r0 + strip
        if r1 < width:
            rest = width - r1

            def trail(k, carry, r0=r0, r1=r1, rest=rest, b=b):
                both = rank_update(w_ref[k, r0:r1, :], z_ref[k, r0:r1, :], width)[r1:]
                w_ref[k, r1:, :] = w_ref[k, r1:, :] - both[:, :width]
                if b == 0:
                    ri = lax.broadcasted_iota(jnp.int32, (rest, width), 0) + r1
                    ci = lax.broadcasted_iota(jnp.int32, (rest, width), 1)
                    old = (ri == ci).astype(jnp.float32)
                else:
                    old = z_ref[k, r1:, :]
                z_ref[k, r1:, :] = old - both[:, width:]
                return carry

            lax.fori_loop(0, n, trail, 0, unroll=True)


def chain_kernel(
    n, width, chain,
    table, gate_tile, sites, sketches,
    out, sums,
    sites_v, sk_v, tab_v, tab_s, gate_v, kept_s, sk_out, sk_b,
    big, st_own, st_in, all_v, acc, prev_w, mat, smp, w_ref, z_ref, tot, wgt,
    load_sem, bar_send, bar_recv, gate_send, gate_recv, sk_send, sk_recv, tr_send, tr_recv,
    own_send, own_recv,
    ed_send, ed_recv, st_send, st_recv, sum_send, sum_recv,
):
    f32 = jnp.float32
    count = 2 * n
    sweeps = 2 * STEPS
    pos = lax.axis_index("site")

    def place(q):
        return q + lax.rem(q, 2) - lax.rem(lax.div(q, 2), 2) if chain % 4 == 0 else q

    me = place(pos)
    bit = lax.rem(pos, 2)
    home = lax.rem(me, 2)
    moved = lax.rem(bit + home, 2)
    is_moved = moved == 1
    after_pos = lax.rem(pos + 1, chain)
    before_pos = lax.rem(pos + chain - 1, chain)
    before_me = lax.rem(me + chain - 1, chain)
    keeps_next = place(after_pos) == pos

    def even_partner(q):
        return q + 1 - 2 * lax.rem(q, 2)

    def odd_partner(q):
        return lax.rem(q - 1 + 2 * lax.rem(q, 2) + chain, chain)

    load_sites = pltpu.make_async_copy(sites, sites_v, load_sem.at[0])
    load_sk = pltpu.make_async_copy(sketches, sk_v, load_sem.at[1])
    load_sites.start()
    load_sk.start()

    barrier = pltpu.get_barrier_semaphore()

    def greet(off, carry):
        pl.semaphore_signal(
            barrier, inc=1, device_id=(lax.rem(pos + off, chain),), device_id_type=MESH
        )
        return carry

    lax.fori_loop(1, chain, greet, 0)
    pl.semaphore_wait(barrier, chain - 1)

    def remote(src, dst, send, recv, to):
        return pltpu.make_async_remote_copy(
            src_ref=src, dst_ref=dst, send_sem=send, recv_sem=recv,
            device_id=(to,), device_id_type=MESH,
        )

    def table_copy(off):
        return remote(
            table, tab_v.at[pos], bar_send.at[off], bar_recv.at[off], lax.rem(pos + off, chain)
        )

    def begin_table(off, carry):
        table_copy(off).start()
        return carry

    def finish_table(off, carry):
        table_copy(off).wait()
        return carry

    lax.fori_loop(1, chain, begin_table, 0)

    def gate_copy(i, to):
        return remote(gate_tile, gate_v.at[i], gate_send.at[i], gate_recv.at[i], to)

    gate_copy(1, after_pos).start()

    @pl.when(is_moved)
    def _():
        gate_copy(2, me).start()

    @pl.when(jnp.logical_not(keeps_next))
    def _():
        gate_copy(3, place(after_pos)).start()

    tab_v[pos] = table[...]
    gate_v[0] = gate_tile[...]

    @pl.when(jnp.logical_not(is_moved))
    def _():
        gate_v[2] = gate_tile[...]

    @pl.when(keeps_next)
    def _():
        gate_v[3] = gate_tile[...]

    lax.fori_loop(1, chain, finish_table, 0)
    to_scalar = pltpu.make_async_copy(tab_v, tab_s, load_sem.at[2])
    to_scalar.start()
    to_scalar.wait()

    def charge_before(site):
        def add_step(d, total):
            return total + jnp.where(d < site, tab_s[d, 0, 2 * count], 0)

        return lax.rem(lax.fori_loop(0, chain, add_step, jnp.int32(0)), count)

    before = charge_before(pos)
    step = tab_s[pos, 0, 2 * count]
    after = before + step
    me_before = charge_before(me)
    me_after = me_before + tab_s[me, 0, 2 * count]

    def wrap(x):
        return lax.rem(x + 2 * count, count)

    row_ids = lax.broadcasted_iota(jnp.int32, (width, width), 0)
    col_ids = lax.broadcasted_iota(jnp.int32, (width, width), 1)
    col_row = lax.broadcasted_iota(jnp.int32, (1, width), 1)
    eye = row_ids == col_ids

    load_sites.wait()

    def block(charge, p):
        label = wrap(charge - before - bit * p)
        target = wrap(label + p - step)
        rows = tab_s[pos, 0, label]
        cols = tab_s[after_pos, 0, target]
        keep = (row_ids < rows) & (col_ids < cols)
        return jnp.where(keep, sites_v[p * count + label], 0.0)

    theirs = (1 - bit) * n

    def trav_copy(t, k, to):
        return remote(
            big.at[OUT, t, k], big.at[IN, t, k], tr_send.at[t, k], tr_recv.at[t, k], to
        )

    def own_copy(k):
        return remote(
            big.at[OWN, sweeps + 1, k], big.at[OWN, 1, k], own_send.at[k], own_recv.at[k], me
        )

    def edge_copy(t, kind, src, slot, k, to):
        return remote(
            big.at[src, slot, k], big.at[kind, t, n], ed_send.at[t, kind], ed_recv.at[t, kind], to
        )

    def stat_copy(t, kind, slot, to):
        return remote(
            st_own.at[slot], st_in.at[kind, t], st_send.at[t, kind], st_recv.at[t, kind], to
        )

    def own_stat_copy():
        return remote(
            st_own.at[sweeps + 1], st_own.at[1], own_send.at[n], own_recv.at[n], me
        )

    for i in range(n):
        k = n - 1 - i + bit * (2 * i - n + 1)
        for p in range(2):
            big[OUT, 0, k, p] = block(theirs + k, p)
        trav_copy(0, k, even_partner(pos)).start()
    for i in range(n):
        k = n - 1 - i
        for p in range(2):
            big[OWN, 0, k, p] = block(bit * n + k, p)
    last_k = n - 1 - bit * (n - 1)
    for p in range(2):
        big[OWN, 0, n, p] = big[OUT, 0, last_k, p]
    edge_copy(0, 1, OWN, 0, last_k, even_partner(pos)).start()

    load_sk.wait()
    for k in range(n):
        label = wrap(theirs + k - after)
        used = col_row < tab_s[pos, 0, count + label]
        sk_out[k] = jnp.where(used, sk_v[label], 0.0)

    def sk_copy(i, src, to):
        return remote(src, sk_b.at[i], sk_send.at[i], sk_recv.at[i], to)

    @pl.when(bit == 0)
    def _():
        sk_copy(1, sk_out, after_pos).start()

    for k in range(n):
        label = wrap(bit * n + k - after)
        kept = tab_s[pos, 0, count + label]
        used = col_row < kept
        sk_b[0, k] = jnp.where(used, sk_v[label], 0.0)
        kept_s[0, k] = kept
        kept_s[1, k] = tab_s[before_pos, 0, count + wrap(bit * n + k - before)]
        kept_s[2, k] = tab_s[me, 0, count + wrap(home * n + k - me_after)]
        kept_s[3, k] = tab_s[before_me, 0, count + wrap(home * n + k - me_before)]

    @pl.when(is_moved)
    def _():
        sk_copy(2, sk_b.at[0], me).start()

    @pl.when(jnp.logical_not(keeps_next))
    def _():
        sk_copy(3, sk_out, place(after_pos)).start()

    @pl.when(jnp.logical_not(is_moved))
    def _():
        for k in range(n):
            sk_b[2, k] = sk_b[0, k]

    @pl.when(keeps_next)
    def _():
        for k in range(n):
            sk_b[3, k] = sk_out[k]

    gate_copy(1, after_pos).wait()

    @pl.when(is_moved)
    def _():
        gate_copy(2, me).wait()

    @pl.when(jnp.logical_not(keeps_next))
    def _():
        gate_copy(3, place(after_pos)).wait()

    tile_rows = lax.broadcasted_iota(jnp.int32, (8, width), 0)
    ones = jnp.where(tile_rows < 2, 0.5, 0.0)
    st_own[0] = ones
    for kind in range(3):
        st_in[kind, 0] = ones
    acc[...] = jnp.zeros_like(acc)
    prev_w[...] = jnp.ones_like(prev_w)

    def fold_stats(t):
        now = st_own[t] + st_in[0, t]
        total, weight = now[0:1], now[1:2]
        acc[0:1] += 1.0 - weight / total
        acc[1:2] += jnp.log(total) - jnp.log(prev_w[0:1])
        return weight

    def one_sweep(t, carry):
        sweep = lax.rem(t, 2)
        first = 1 - lax.div(t + sweeps - 1, sweeps)
        last = lax.div(t, sweeps - 1)
        q = first * pos + (1 - first) * me
        half = lax.rem(q, 2)
        odd = half == 1
        is_left = half == sweep
        first_moved = (t == 0) & is_moved
        second_moved = (t == 1) & is_moved

        def kk(i):
            return i + half * (n - 1 - 2 * i)

        def jj(m):
            return m + half * (n - 2 * m)

        which = lax.rem(half + sweep, 2)
        left_in, right_in = which, 1 - which
        own_kind = OUT * last * moved
        trav_kind = OUT - own_kind
        own_slot = t + 1 + first * moved * sweeps
        left_out = own_kind + which * (trav_kind - own_kind)
        right_out = OUT - left_out
        left_slot = own_slot + which * (t + 1 - own_slot)
        right_slot = own_slot + t + 1 - left_slot
        table_row = which + 2 * (1 - first)
        idle = (sweep == 1) & ((q == 0) | (q == chain - 1))
        first_edge = sweep

        def left_block(m):
            if m == 0:
                return n - half
            return n - 1 + half if m == n else jj(m) - 1

        ends = last * (moved * me + (1 - moved) * odd_partner(q))
        by = 2 - 4 * lax.rem(q + t, 2)
        travel = ends + (1 - last) * place(lax.rem(q + by + chain, chain))
        even_to = place(even_partner(q))
        odd_to = place(odd_partner(q))

        def send_blocks(group):
            for i in group:
                trav_copy(t + 1, kk(i), travel).start()

            @pl.when(first_moved)
            def _():
                for i in group:
                    own_copy(kk(i)).start()

            if group[0] == 0:
                k = kk(0)

                @pl.when(first_moved)
                def _():
                    for p in range(2):
                        big[IN, 1, n, p] = big[OWN, sweeps + 1, k, p]

                @pl.when((t < sweeps - 1) & jnp.logical_not(first_moved))
                def _():
                    edge_copy(t + 1, 1 - sweep, OUT * sweep, t + 1, k, odd_to).start()

            if group[-1] == n - 1:

                @pl.when(t < sweeps - 1)
                def _():
                    edge_copy(t + 1, sweep, OUT * (1 - sweep), t + 1, kk(n - 1), even_to).start()

        def send_stats():
            near = even_to + sweep * (odd_to - even_to)
            far = odd_to + even_to - near
            stat_copy(t + 1, 0, own_slot, near).start()

            @pl.when(t < sweeps - 1)
            def _():
                stat_copy(t + 1, 1, own_slot, travel).start()

            @pl.when((t < sweeps - 1) & jnp.logical_not(first_moved))
            def _():
                stat_copy(t + 1, 2, own_slot, far).start()

            @pl.when(first_moved)
            def _():
                own_stat_copy().start()
                st_in[2, 1] = st_own[sweeps + 1]

        def wait_blocks(group):
            if group[0] == 0:

                @pl.when((t > 0) & jnp.logical_not(second_moved))
                def _():
                    edge_copy(t, first_edge, OWN, 0, 0, even_to).wait_recv()

            for m in group:
                if m < n:
                    trav_copy(t, kk(m), even_to).wait_recv()

            @pl.when(second_moved)
            def _():
                for m in group:
                    if m < n:
                        own_copy(kk(m)).wait_recv()

            if group[-1] == n:
                edge_copy(t, 1 - first_edge, OWN, 0, 0, even_to).wait_recv()

        def wait_stats():
            @pl.when(t > 0)
            def _():
                for kind in range(2):
                    stat_copy(t, kind, 0, even_to).wait_recv()

            @pl.when((t > 0) & jnp.logical_not(second_moved))
            def _():
                stat_copy(t, 2, 0, even_to).wait_recv()

            @pl.when(second_moved)
            def _():
                own_stat_copy().wait_recv()

            weight = fold_stats(t)
            other = st_in[1, t][1:2] + st_in[2, t][1:2]
            return jnp.where(is_left, weight, other)

        def stats(total, weight):
            st_own[own_slot] = jnp.where(tile_rows == 0, total, jnp.where(tile_rows == 1, weight, 0.0))

        early = (t > 0) & (t < 3)

        @pl.when((t == 0) & (half == 1))
        def _():
            sk_copy(1, sk_out, even_to).wait_recv()

        @pl.when(early & is_left & is_moved)
        def _():
            sk_copy(2, sk_out, even_to).wait_recv()

        @pl.when(early & jnp.logical_not(is_left) & jnp.logical_not(keeps_next))
        def _():
            sk_copy(3, sk_out, even_to).wait_recv()

        @pl.when(idle)
        def _():
            wait_blocks(range(n + 1))
            left_w = wait_stats()
            scale = 1.0 / jnp.sqrt(left_w)
            for i in range(n):
                k = kk(i)
                below = n - 2 * half if i == 0 else n - 2 + 2 * half if i == n - 1 else k - 1
                big[left_out, left_slot, k, 0] = scale * big[left_in, t, k, 0]
                big[left_out, left_slot, k, 1] = scale * big[left_in, t, below, 1]
                big[right_out, right_slot, k, 0] = big[right_in, t, k, 0]
                big[right_out, right_slot, k, 1] = big[right_in, t, k + 1, 1]
            send_blocks(range(n))
            stats(0.5, 0.5)
            send_stats()
            prev_w[...] = jnp.ones_like(prev_w)

        @pl.when(jnp.logical_not(idle))
        def _():
            g = [gate_v[table_row, 0:1, i : i + 1] for i in range(6)]
            tot[...] = jnp.zeros_like(tot)
            wgt[...] = jnp.zeros_like(wgt)

            def load(m):
                jl = left_block(m)
                return (
                    [big[left_in, t, jl, p] for p in range(2)],
                    [big[right_in, t, jj(m), p] for p in range(2)],
                )

            def mixes(m):
                j = jj(m)
                lx, rx = load(m)
                s01 = mm(lx[0], rx[1])
                s10 = mm(lx[1], rx[0])
                mat[j, :width, width:] = g[2] * s01 + g[3] * s10
                mat[j + 1, width:, :width] = g[4] * s01 + g[5] * s10

            def diagonals(m):
                k = kk(m - 1)
                plx, prx = load(m - 1)
                lx, rx = load(m)
                l0 = jnp.where(odd, plx[0], lx[0])
                l1 = jnp.where(odd, lx[1], plx[1])
                r0 = jnp.where(odd, rx[0], prx[0])
                r1 = jnp.where(odd, prx[1], rx[1])
                mat[k + 1, :width, :width] = g[0] * mm(l0, r0)
                mat[k + 1, width:, width:] = g[1] * mm(l1, r1)

            def sample(i):
                k = kk(i)
                mk = mat[k + 1]
                sq = jnp.sum(mk * mk, axis=0, keepdims=True)
                tot[0:1, :] += sq[:, :width] + sq[:, width:]
                smp[k] = mm(mk, sk_b[table_row, k])

            def gram(i):
                k = kk(i)
                s = smp[k]
                w_ref[k] = mm(s, s, 0, 0)

            for group in groups_of(n + 1, TAKE):
                wait_blocks(group)
                for m in group:
                    mixes(m)
                for m in group:
                    if m > 0:
                        diagonals(m)
                for m in group:
                    if m > 0:
                        sample(m - 1)
                for m in group:
                    if m > 0:
                        gram(m - 1)

            left_w = wait_stats()
            for k in range(n):
                s = smp[k]
                used = col_row < kept_s[table_row, k]
                ds = jnp.sum(jnp.sum(s * s, axis=0, keepdims=True), axis=1, keepdims=True)
                kf = kept_s[table_row, k].astype(f32)
                ridge = 0.001 * ds / kf + 1e-06 * left_w
                add = ridge + jnp.where(used, 0.0, 1.0)
                w_ref[k] = w_ref[k] + jnp.where(eye, add, 0.0)
            inverse_factors(w_ref, z_ref, n, width)

            for group in groups_of(n, GIVE):
                reds = []
                for i in group:
                    k = kk(i)
                    basis = mm(smp[k], z_ref[k], 1, 1)
                    for p in range(2):
                        big[left_out, left_slot, k, p] = basis[p * width : (p + 1) * width]
                    reds.append(basis)
                for i, basis in zip(group, reds):
                    k = kk(i)
                    red = mm(basis, mat[k + 1], 0, 0)
                    sq = jnp.sum(red * red, axis=0, keepdims=True)
                    wgt[0:1, :] += sq[:, :width] + sq[:, width:]
                    for p in range(2):
                        big[right_out, right_slot, k, p] = red[:, p * width : (p + 1) * width]
                send_blocks(group)
            stats(
                jnp.sum(tot[0:1, :], axis=1, keepdims=True),
                jnp.sum(wgt[0:1, :], axis=1, keepdims=True),
            )
            send_stats()
            prev_w[...] = jnp.broadcast_to(left_w, prev_w.shape)

        return carry

    lax.fori_loop(0, sweeps, one_sweep, 0)

    stat_copy(sweeps, 0, 0, after_pos).wait_recv()
    weight = fold_stats(sweeps)
    all_v[pos] = 0.5 * acc[...]

    def sum_copy(off):
        return remote(
            all_v.at[pos], all_v.at[pos], sum_send.at[off], sum_recv.at[off],
            lax.rem(pos + off, chain),
        )

    def begin_sum(off, carry):
        sum_copy(off).start()
        return carry

    def finish_sum(off, carry):
        sum_copy(off).wait()
        return carry

    lax.fori_loop(1, chain, begin_sum, 0)
    scale = jnp.where(bit == 1, 1.0, 1.0 / jnp.sqrt(weight))
    for k in range(n):
        trav_copy(sweeps, k, after_pos).wait_recv()
    for p in range(2):
        for l in range(count):
            index = wrap(l + before + bit * p + home * n)
            far = (index >= n).astype(jnp.int32)
            out[p * count + l] = big[far, sweeps, index - n * far, p] * scale
    lax.fori_loop(1, chain, finish_sum, 0)
    sums[...] = jnp.sum(all_v[...], axis=0)

    @pl.when(bit == 0)
    def _():
        sk_copy(1, sk_out, after_pos).wait_send()

    @pl.when(jnp.logical_not(keeps_next))
    def _():
        sk_copy(3, sk_out, after_pos).wait_send()

    @pl.when(is_moved)
    def _():
        sk_copy(2, sk_out, after_pos).wait_send()
        own_stat_copy().wait_send()
        for k in range(n):
            own_copy(k).wait_send()

    edge_copy(0, 1, OWN, 0, 0, after_pos).wait_send()

    def drain(t, carry):
        for k in range(n):
            trav_copy(t, k, after_pos).wait_send()

        inner = (t > 0) & (t < sweeps)
        here = (t == 1) & is_moved

        @pl.when(inner)
        def _():
            edge_copy(t, 0, OWN, 0, 0, after_pos).wait_send()
            stat_copy(t, 1, 0, after_pos).wait_send()

        @pl.when(inner & jnp.logical_not(here))
        def _():
            edge_copy(t, 1, OWN, 0, 0, after_pos).wait_send()
            stat_copy(t, 2, 0, after_pos).wait_send()

        @pl.when(t > 0)
        def _():
            stat_copy(t, 0, 0, after_pos).wait_send()

        return carry

    lax.fori_loop(0, sweeps + 1, drain, 0)


def run_chain(n, width, chain, table, gate_tile, sites, sketches):
    f32, i32 = jnp.float32, jnp.int32
    count, slots = 2 * n, 2 * STEPS + 1
    vmem = pl.BlockSpec(memory_space=pltpu.VMEM)
    anywhere = pl.BlockSpec(memory_space=pl.ANY)
    dma = pltpu.SemaphoreType.DMA
    return pl.pallas_call(
        functools.partial(chain_kernel, n, width, chain),
        out_shape=(
            jax.ShapeDtypeStruct((2 * count, width, width), f32),
            jax.ShapeDtypeStruct((8, width), f32),
        ),
        in_specs=[vmem, vmem, anywhere, anywhere],
        out_specs=(vmem, vmem),
        scratch_shapes=[
            pltpu.VMEM((2 * count, width, width), f32),
            pltpu.VMEM((count, 2 * width, width), f32),
            pltpu.VMEM((chain, 1, width), i32),
            pltpu.SMEM((chain, 1, width), i32),
            pltpu.VMEM((4, 8, width), f32),
            pltpu.SMEM((4, n), i32),
            pltpu.VMEM((n, 2 * width, width), f32),
            pltpu.VMEM((4, n, 2 * width, width), f32),
            pltpu.VMEM((3, slots + 1, n + 1, 2, width, width), f32),
            pltpu.VMEM((slots + 1, 8, width), f32),
            pltpu.VMEM((3, slots, 8, width), f32),
            pltpu.VMEM((chain, 8, width), f32),
            pltpu.VMEM((8, width), f32),
            pltpu.VMEM((8, width), f32),
            pltpu.VMEM((n + 2, 2 * width, 2 * width), f32),
            pltpu.VMEM((n, 2 * width, width), f32),
            pltpu.VMEM((n, width, width), f32),
            pltpu.VMEM((n, width, width), f32),
            pltpu.VMEM((8, width), f32),
            pltpu.VMEM((8, width), f32),
            dma((3,)),
            dma((chain,)),
            dma((chain,)),
            dma((4,)),
            dma((4,)),
            dma((4,)),
            dma((4,)),
            dma((slots, n)),
            dma((slots, n)),
            dma((n + 1,)),
            dma((n + 1,)),
            dma((slots, 2)),
            dma((slots, 2)),
            dma((slots, 3)),
            dma((slots, 3)),
            dma((chain,)),
            dma((chain,)),
        ],
        compiler_params=pltpu.CompilerParams(
            collective_id=1, has_side_effects=True, vmem_limit_bytes=56 * 1024 * 1024
        ),
    )(table, gate_tile, sites, sketches)


def body(sites, sector_sizes, charge_steps, kept_counts, gates, sketches):
    chain = lax.axis_size("site")
    count, width = sites.shape[2], sites.shape[-1]
    n = count // 2
    table = jnp.concatenate([sector_sizes, kept_counts, charge_steps[:, None]], axis=1)
    table = jnp.pad(table, ((0, 0), (0, width - table.shape[1])))
    gate_tile = jnp.pad(gates, ((0, 7), (0, width - gates.shape[1])))
    out, sums = run_chain(
        n, width, chain, table, gate_tile,
        sites.reshape(2 * count, width, width), sketches.reshape(count, 2 * width, width),
    )
    return out.reshape(sites.shape), sums[:2, 0]


def solution(mesh):
    placed = (
        P("site", None, None, None, None),
        P("site", None),
        P("site"),
        P("site", None),
        P("site", None),
        P("site", None, None, None),
    )
    return jax.shard_map(
        body,
        mesh=mesh,
        in_specs=placed,
        out_specs=(P("site", None, None, None, None), P()),
        check_vma=False,
    )
```

```python
import functools

import jax
import jax.numpy as jnp
from jax import lax
from jax.experimental import pallas as pl
from jax.experimental.pallas import tpu as pltpu
from jax.sharding import PartitionSpec as P

STEPS = 4
HI = lax.Precision.HIGHEST
MESH = pl.DeviceIdType.MESH
OWN, IN, OUT = 0, 1, 2
TAKE, GIVE = (3, 2), (2, 2)


def groups_of(total, sizes):
    out, at = [], 0
    while at < total:
        size = sizes[min(len(out), len(sizes) - 1)]
        out.append(range(at, min(at + size, total)))
        at += size
    return out


def mm(a, b, ca=1, cb=0):
    return lax.dot_general(
        a, b, (((ca,), (cb,)), ((), ())), precision=HI, preferred_element_type=jnp.float32
    )


def split3(a):
    bf16, f32 = jnp.bfloat16, jnp.float32
    a1 = a.astype(bf16)
    rest = a - a1.astype(f32)
    a2 = rest.astype(bf16)
    return a1, a2, (rest - a2.astype(f32)).astype(bf16)


def rank_update(pk, zk, width):
    b1, b2, b3 = split3(jnp.concatenate([pk, zk], axis=1))
    a1, a2, a3 = (b[:, :width] for b in (b1, b2, b3))
    return lax.dot_general(
        jnp.concatenate([a3, a1, a2, a2, a1, a1], axis=0),
        jnp.concatenate([b1, b3, b2, b1, b2, b1], axis=0),
        (((0,), (0,)), ((), ())), preferred_element_type=jnp.float32,
    )


def inverse_factors(w_ref, z_ref, n, width):
    strip, ahead = 32, 4
    lanes = lax.broadcasted_iota(jnp.int32, (1, 8, width), 2)
    subs = lax.broadcasted_iota(jnp.int32, (1, 8, width), 1)
    for b in range(width // strip):
        r0 = b * strip
        groups = strip // 8
        ps = [w_ref[:, r0 + 8 * g : r0 + 8 * g + 8, :] for g in range(groups)]
        if b == 0:
            zs = [
                jnp.broadcast_to((lanes == subs + 8 * g).astype(jnp.float32), ps[0].shape)
                for g in range(groups)
            ]
        else:
            zs = [z_ref[:, r0 + 8 * g : r0 + 8 * g + 8, :] for g in range(groups)]
        for q in range(groups):
            root = jnp.zeros_like(ps[q])
            for h in range(0, 8, ahead):
                c0 = r0 + 8 * q + h
                vs = [
                    [
                        jnp.broadcast_to(ps[g][:, :, c0 + t : c0 + t + 1], ps[g].shape)
                        if g >= q
                        else None
                        for g in range(groups)
                    ]
                    for t in range(ahead)
                ]
                for t in range(ahead):
                    row = h + t
                    piv = vs[t][q][:, row : row + 1, :]
                    inv = lax.rsqrt(piv)
                    inv = inv * (1.5 - 0.5 * piv * inv * inv)
                    inv2 = inv * inv
                    root = jnp.where(subs == row, inv, root)
                    below = jnp.where(subs > row, vs[t][q], 0.0)

                    def eliminate(rows):
                        scaled = rows[q][:, row : row + 1, :] * inv2
                        out = list(rows)
                        if row < 7:
                            out[q] = rows[q] - below * scaled
                        for g in range(q + 1, groups):
                            out[g] = rows[g] - vs[t][g] * scaled
                        return out

                    ps = eliminate(ps)
                    zs = eliminate(zs)
                    for t2 in range(t + 1, ahead):
                        vs[t2] = eliminate(vs[t2])
            ps[q] = ps[q] * root
            zs[q] = zs[q] * root
        for g in range(groups):
            z_ref[:, r0 + 8 * g : r0 + 8 * g + 8, :] = zs[g]
            w_ref[:, r0 + 8 * g : r0 + 8 * g + 8, :] = ps[g]
        r1 = r0 + strip
        if r1 < width:
            rest = width - r1

            def trail(k, carry, r0=r0, r1=r1, rest=rest, b=b):
                both = rank_update(w_ref[k, r0:r1, :], z_ref[k, r0:r1, :], width)[r1:]
                w_ref[k, r1:, :] = w_ref[k, r1:, :] - both[:, :width]
                if b == 0:
                    ri = lax.broadcasted_iota(jnp.int32, (rest, width), 0) + r1
                    ci = lax.broadcasted_iota(jnp.int32, (rest, width), 1)
                    old = (ri == ci).astype(jnp.float32)
                else:
                    old = z_ref[k, r1:, :]
                z_ref[k, r1:, :] = old - both[:, width:]
                return carry

            lax.fori_loop(0, n, trail, 0, unroll=True)


def chain_kernel(
    n, width, chain,
    table, gate_tile, sites, sketches,
    out, sums,
    sites_v, sk_v, tab_v, tab_s, gate_v, kept_s, sk_out, sk_b,
    big, st_own, st_in, all_v, acc, prev_w, mat, smp, w_ref, z_ref, tot, wgt,
    load_sem, bar_send, bar_recv, gate_send, gate_recv, sk_send, sk_recv, tr_send, tr_recv,
    own_send, own_recv,
    ed_send, ed_recv, st_send, st_recv, sum_send, sum_recv,
):
    f32 = jnp.float32
    count = 2 * n
    sweeps = 2 * STEPS
    pos = lax.axis_index("site")

    def place(q):
        return q + lax.rem(q, 2) - lax.rem(lax.div(q, 2), 2) if chain % 4 == 0 else q

    me = place(pos)
    bit = lax.rem(pos, 2)
    home = lax.rem(me, 2)
    moved = lax.rem(bit + home, 2)
    is_moved = moved == 1
    after_pos = lax.rem(pos + 1, chain)
    before_pos = lax.rem(pos + chain - 1, chain)
    before_me = lax.rem(me + chain - 1, chain)
    keeps_next = place(after_pos) == pos

    def even_partner(q):
        return q + 1 - 2 * lax.rem(q, 2)

    def odd_partner(q):
        return lax.rem(q - 1 + 2 * lax.rem(q, 2) + chain, chain)

    load_sites = pltpu.make_async_copy(sites, sites_v, load_sem.at[0])
    load_sk = pltpu.make_async_copy(sketches, sk_v, load_sem.at[1])
    load_sites.start()
    load_sk.start()

    barrier = pltpu.get_barrier_semaphore()

    def greet(off, carry):
        pl.semaphore_signal(
            barrier, inc=1, device_id=(lax.rem(pos + off, chain),), device_id_type=MESH
        )
        return carry

    lax.fori_loop(1, chain, greet, 0)
    pl.semaphore_wait(barrier, chain - 1)

    def remote(src, dst, send, recv, to):
        return pltpu.make_async_remote_copy(
            src_ref=src, dst_ref=dst, send_sem=send, recv_sem=recv,
            device_id=(to,), device_id_type=MESH,
        )

    def table_copy(off):
        return remote(
            table, tab_v.at[pos], bar_send.at[off], bar_recv.at[off], lax.rem(pos + off, chain)
        )

    def begin_table(off, carry):
        table_copy(off).start()
        return carry

    def finish_table(off, carry):
        table_copy(off).wait()
        return carry

    lax.fori_loop(1, chain, begin_table, 0)

    def gate_copy(i, to):
        return remote(gate_tile, gate_v.at[i], gate_send.at[i], gate_recv.at[i], to)

    gate_copy(1, after_pos).start()

    @pl.when(is_moved)
    def _():
        gate_copy(2, me).start()

    @pl.when(jnp.logical_not(keeps_next))
    def _():
        gate_copy(3, place(after_pos)).start()

    tab_v[pos] = table[...]
    gate_v[0] = gate_tile[...]

    @pl.when(jnp.logical_not(is_moved))
    def _():
        gate_v[2] = gate_tile[...]

    @pl.when(keeps_next)
    def _():
        gate_v[3] = gate_tile[...]

    lax.fori_loop(1, chain, finish_table, 0)
    to_scalar = pltpu.make_async_copy(tab_v, tab_s, load_sem.at[2])
    to_scalar.start()
    to_scalar.wait()

    def charge_before(site):
        def add_step(d, total):
            return total + jnp.where(d < site, tab_s[d, 0, 2 * count], 0)

        return lax.rem(lax.fori_loop(0, chain, add_step, jnp.int32(0)), count)

    before = charge_before(pos)
    step = tab_s[pos, 0, 2 * count]
    after = before + step
    me_before = charge_before(me)
    me_after = me_before + tab_s[me, 0, 2 * count]

    def wrap(x):
        return lax.rem(x + 2 * count, count)

    row_ids = lax.broadcasted_iota(jnp.int32, (width, width), 0)
    col_ids = lax.broadcasted_iota(jnp.int32, (width, width), 1)
    col_row = lax.broadcasted_iota(jnp.int32, (1, width), 1)
    eye = row_ids == col_ids

    load_sites.wait()

    def block(charge, p):
        label = wrap(charge - before - bit * p)
        target = wrap(label + p - step)
        rows = tab_s[pos, 0, label]
        cols = tab_s[after_pos, 0, target]
        keep = (row_ids < rows) & (col_ids < cols)
        return jnp.where(keep, sites_v[p * count + label], 0.0)

    theirs = (1 - bit) * n

    def trav_copy(t, k, to):
        return remote(
            big.at[OUT, t, k], big.at[IN, t, k], tr_send.at[t, k], tr_recv.at[t, k], to
        )

    def own_copy(k):
        return remote(
            big.at[OWN, sweeps + 1, k], big.at[OWN, 1, k], own_send.at[k], own_recv.at[k], me
        )

    def edge_copy(t, kind, src, slot, k, to):
        return remote(
            big.at[src, slot, k], big.at[kind, t, n], ed_send.at[t, kind], ed_recv.at[t, kind], to
        )

    def stat_copy(t, kind, slot, to):
        return remote(
            st_own.at[slot], st_in.at[kind, t], st_send.at[t, kind], st_recv.at[t, kind], to
        )

    def own_stat_copy():
        return remote(
            st_own.at[sweeps + 1], st_own.at[1], own_send.at[n], own_recv.at[n], me
        )

    for i in range(n):
        k = n - 1 - i + bit * (2 * i - n + 1)
        for p in range(2):
            big[OUT, 0, k, p] = block(theirs + k, p)
        trav_copy(0, k, even_partner(pos)).start()
    for i in range(n):
        k = n - 1 - i
        for p in range(2):
            big[OWN, 0, k, p] = block(bit * n + k, p)
    last_k = n - 1 - bit * (n - 1)
    for p in range(2):
        big[OWN, 0, n, p] = big[OUT, 0, last_k, p]
    edge_copy(0, 1, OWN, 0, last_k, even_partner(pos)).start()

    load_sk.wait()
    for k in range(n):
        label = wrap(theirs + k - after)
        used = col_row < tab_s[pos, 0, count + label]
        sk_out[k] = jnp.where(used, sk_v[label], 0.0)

    def sk_copy(i, src, to):
        return remote(src, sk_b.at[i], sk_send.at[i], sk_recv.at[i], to)

    @pl.when(bit == 0)
    def _():
        sk_copy(1, sk_out, after_pos).start()

    for k in range(n):
        label = wrap(bit * n + k - after)
        kept = tab_s[pos, 0, count + label]
        used = col_row < kept
        sk_b[0, k] = jnp.where(used, sk_v[label], 0.0)
        kept_s[0, k] = kept
        kept_s[1, k] = tab_s[before_pos, 0, count + wrap(bit * n + k - before)]
        kept_s[2, k] = tab_s[me, 0, count + wrap(home * n + k - me_after)]
        kept_s[3, k] = tab_s[before_me, 0, count + wrap(home * n + k - me_before)]

    @pl.when(is_moved)
    def _():
        sk_copy(2, sk_b.at[0], me).start()

    @pl.when(jnp.logical_not(keeps_next))
    def _():
        sk_copy(3, sk_out, place(after_pos)).start()

    @pl.when(jnp.logical_not(is_moved))
    def _():
        for k in range(n):
            sk_b[2, k] = sk_b[0, k]

    @pl.when(keeps_next)
    def _():
        for k in range(n):
            sk_b[3, k] = sk_out[k]

    gate_copy(1, after_pos).wait()

    @pl.when(is_moved)
    def _():
        gate_copy(2, me).wait()

    @pl.when(jnp.logical_not(keeps_next))
    def _():
        gate_copy(3, place(after_pos)).wait()

    tile_rows = lax.broadcasted_iota(jnp.int32, (8, width), 0)
    ones = jnp.where(tile_rows < 2, 0.5, 0.0)
    st_own[0] = ones
    for kind in range(3):
        st_in[kind, 0] = ones
    acc[...] = jnp.zeros_like(acc)
    prev_w[...] = jnp.ones_like(prev_w)

    def fold_stats(t):
        now = st_own[t] + st_in[0, t]
        total, weight = now[0:1], now[1:2]
        acc[0:1] += 1.0 - weight / total
        acc[1:2] += jnp.log(total) - jnp.log(prev_w[0:1])
        return weight

    def one_sweep(t, carry):
        sweep = lax.rem(t, 2)
        first = 1 - lax.div(t + sweeps - 1, sweeps)
        last = lax.div(t, sweeps - 1)
        q = first * pos + (1 - first) * me
        half = lax.rem(q, 2)
        is_left = half == sweep
        first_moved = (t == 0) & is_moved
        second_moved = (t == 1) & is_moved

        def kk(i):
            return i + half * (n - 1 - 2 * i)

        def jj(m):
            return m + half * (n - 2 * m)

        which = lax.rem(half + sweep, 2)
        left_in, right_in = which, 1 - which
        own_kind = OUT * last * moved
        trav_kind = OUT - own_kind
        own_slot = t + 1 + first * moved * sweeps
        left_out = own_kind + which * (trav_kind - own_kind)
        right_out = OUT - left_out
        left_slot = own_slot + which * (t + 1 - own_slot)
        right_slot = own_slot + t + 1 - left_slot
        table_row = which + 2 * (1 - first)
        idle = (sweep == 1) & ((q == 0) | (q == chain - 1))
        first_edge = sweep

        def left_block(m):
            if m == 0:
                return n - half
            return n - 1 + half if m == n else jj(m) - 1

        ends = last * (moved * me + (1 - moved) * odd_partner(q))
        by = 2 - 4 * lax.rem(q + t, 2)
        travel = ends + (1 - last) * place(lax.rem(q + by + chain, chain))
        even_to = place(even_partner(q))
        odd_to = place(odd_partner(q))

        def send_blocks(group):
            for i in group:
                trav_copy(t + 1, kk(i), travel).start()

            @pl.when(first_moved)
            def _():
                for i in group:
                    own_copy(kk(i)).start()

            if group[0] == 0:
                k = kk(0)

                @pl.when(first_moved)
                def _():
                    for p in range(2):
                        big[IN, 1, n, p] = big[OWN, sweeps + 1, k, p]

                @pl.when((t < sweeps - 1) & jnp.logical_not(first_moved))
                def _():
                    edge_copy(t + 1, 1 - sweep, OUT * sweep, t + 1, k, odd_to).start()

            if group[-1] == n - 1:

                @pl.when(t < sweeps - 1)
                def _():
                    edge_copy(t + 1, sweep, OUT * (1 - sweep), t + 1, kk(n - 1), even_to).start()

        def send_stats():
            near = even_to + sweep * (odd_to - even_to)
            far = odd_to + even_to - near
            stat_copy(t + 1, 0, own_slot, near).start()

            @pl.when(t < sweeps - 1)
            def _():
                stat_copy(t + 1, 1, own_slot, travel).start()

            @pl.when((t < sweeps - 1) & jnp.logical_not(first_moved))
            def _():
                stat_copy(t + 1, 2, own_slot, far).start()

            @pl.when(first_moved)
            def _():
                own_stat_copy().start()
                st_in[2, 1] = st_own[sweeps + 1]

        def wait_blocks(group):
            if group[0] == 0:

                @pl.when((t > 0) & jnp.logical_not(second_moved))
                def _():
                    edge_copy(t, first_edge, OWN, 0, 0, even_to).wait_recv()

            for m in group:
                if m < n:
                    trav_copy(t, kk(m), even_to).wait_recv()

            @pl.when(second_moved)
            def _():
                for m in group:
                    if m < n:
                        own_copy(kk(m)).wait_recv()

            if group[-1] == n:
                edge_copy(t, 1 - first_edge, OWN, 0, 0, even_to).wait_recv()

        def wait_stats():
            @pl.when(t > 0)
            def _():
                for kind in range(2):
                    stat_copy(t, kind, 0, even_to).wait_recv()

            @pl.when((t > 0) & jnp.logical_not(second_moved))
            def _():
                stat_copy(t, 2, 0, even_to).wait_recv()

            @pl.when(second_moved)
            def _():
                own_stat_copy().wait_recv()

            weight = fold_stats(t)
            other = st_in[1, t][1:2] + st_in[2, t][1:2]
            return jnp.where(is_left, weight, other)

        def stats(total, weight):
            st_own[own_slot] = jnp.where(tile_rows == 0, total, jnp.where(tile_rows == 1, weight, 0.0))

        early = (t > 0) & (t < 3)

        @pl.when((t == 0) & (half == 1))
        def _():
            sk_copy(1, sk_out, even_to).wait_recv()

        @pl.when(early & is_left & is_moved)
        def _():
            sk_copy(2, sk_out, even_to).wait_recv()

        @pl.when(early & jnp.logical_not(is_left) & jnp.logical_not(keeps_next))
        def _():
            sk_copy(3, sk_out, even_to).wait_recv()

        @pl.when(idle)
        def _():
            wait_blocks(range(n + 1))
            left_w = wait_stats()
            scale = 1.0 / jnp.sqrt(left_w)
            for i in range(n):
                k = kk(i)
                below = n - 2 * half if i == 0 else n - 2 + 2 * half if i == n - 1 else k - 1
                big[left_out, left_slot, k, 0] = scale * big[left_in, t, k, 0]
                big[left_out, left_slot, k, 1] = scale * big[left_in, t, below, 1]
                big[right_out, right_slot, k, 0] = big[right_in, t, k, 0]
                big[right_out, right_slot, k, 1] = big[right_in, t, k + 1, 1]
            send_blocks(range(n))
            stats(0.5, 0.5)
            send_stats()
            prev_w[...] = jnp.ones_like(prev_w)

        @pl.when(jnp.logical_not(idle))
        def _():
            g = [gate_v[table_row, 0:1, i : i + 1] for i in range(6)]
            tot[...] = jnp.zeros_like(tot)
            wgt[...] = jnp.zeros_like(wgt)

            def mixes(m):
                j = jj(m)
                jl = left_block(m)
                s01 = mm(big[left_in, t, jl, 0], big[right_in, t, j, 1])
                s10 = mm(big[left_in, t, jl, 1], big[right_in, t, j, 0])
                mat[j, :width, width:] = g[2] * s01 + g[3] * s10
                mat[j + 1, width:, :width] = g[4] * s01 + g[5] * s10

            def diagonals(m):
                k = kk(m - 1)
                below = n - 2 * half if m == 1 else n - 2 + 2 * half if m == n else k - 1
                mat[k + 1, :width, :width] = g[0] * mm(
                    big[left_in, t, k, 0], big[right_in, t, k, 0]
                )
                mat[k + 1, width:, width:] = g[1] * mm(
                    big[left_in, t, below, 1], big[right_in, t, k + 1, 1]
                )

            def sample(i):
                k = kk(i)
                mk = mat[k + 1]
                sq = jnp.sum(mk * mk, axis=0, keepdims=True)
                tot[0:1, :] += sq[:, :width] + sq[:, width:]
                smp[k] = mm(mk, sk_b[table_row, k])

            def gram(i):
                k = kk(i)
                s = smp[k]
                w_ref[k] = mm(s, s, 0, 0)

            for group in groups_of(n + 1, TAKE):
                wait_blocks(group)
                for m in group:
                    mixes(m)
                for m in group:
                    if m > 0:
                        diagonals(m)
                for m in group:
                    if m > 0:
                        sample(m - 1)
                for m in group:
                    if m > 0:
                        gram(m - 1)

            left_w = wait_stats()
            for k in range(n):
                s = smp[k]
                used = col_row < kept_s[table_row, k]
                ds = jnp.sum(jnp.sum(s * s, axis=0, keepdims=True), axis=1, keepdims=True)
                kf = kept_s[table_row, k].astype(f32)
                ridge = 0.001 * ds / kf + 1e-06 * left_w
                add = ridge + jnp.where(used, 0.0, 1.0)
                w_ref[k] = w_ref[k] + jnp.where(eye, add, 0.0)
            inverse_factors(w_ref, z_ref, n, width)

            for group in groups_of(n, GIVE):
                reds = []
                for i in group:
                    k = kk(i)
                    basis = mm(smp[k], z_ref[k], 1, 1)
                    for p in range(2):
                        big[left_out, left_slot, k, p] = basis[p * width : (p + 1) * width]
                    reds.append(basis)
                for i, basis in zip(group, reds):
                    k = kk(i)
                    red = mm(basis, mat[k + 1], 0, 0)
                    sq = jnp.sum(red * red, axis=0, keepdims=True)
                    wgt[0:1, :] += sq[:, :width] + sq[:, width:]
                    for p in range(2):
                        big[right_out, right_slot, k, p] = red[:, p * width : (p + 1) * width]
                send_blocks(group)
            stats(
                jnp.sum(tot[0:1, :], axis=1, keepdims=True),
                jnp.sum(wgt[0:1, :], axis=1, keepdims=True),
            )
            send_stats()
            prev_w[...] = jnp.broadcast_to(left_w, prev_w.shape)

        return carry

    lax.fori_loop(0, sweeps, one_sweep, 0)

    stat_copy(sweeps, 0, 0, after_pos).wait_recv()
    weight = fold_stats(sweeps)
    all_v[pos] = 0.5 * acc[...]

    def sum_copy(off):
        return remote(
            all_v.at[pos], all_v.at[pos], sum_send.at[off], sum_recv.at[off],
            lax.rem(pos + off, chain),
        )

    def begin_sum(off, carry):
        sum_copy(off).start()
        return carry

    def finish_sum(off, carry):
        sum_copy(off).wait()
        return carry

    lax.fori_loop(1, chain, begin_sum, 0)
    scale = jnp.where(bit == 1, 1.0, 1.0 / jnp.sqrt(weight))
    for k in range(n):
        trav_copy(sweeps, k, after_pos).wait_recv()
    for p in range(2):
        for l in range(count):
            index = wrap(l + before + bit * p + home * n)
            far = (index >= n).astype(jnp.int32)
            out[p * count + l] = big[far, sweeps, index - n * far, p] * scale
    lax.fori_loop(1, chain, finish_sum, 0)
    sums[...] = jnp.sum(all_v[...], axis=0)

    @pl.when(bit == 0)
    def _():
        sk_copy(1, sk_out, after_pos).wait_send()

    @pl.when(jnp.logical_not(keeps_next))
    def _():
        sk_copy(3, sk_out, after_pos).wait_send()

    @pl.when(is_moved)
    def _():
        sk_copy(2, sk_out, after_pos).wait_send()
        own_stat_copy().wait_send()
        for k in range(n):
            own_copy(k).wait_send()

    edge_copy(0, 1, OWN, 0, 0, after_pos).wait_send()

    def drain(t, carry):
        for k in range(n):
            trav_copy(t, k, after_pos).wait_send()

        inner = (t > 0) & (t < sweeps)
        here = (t == 1) & is_moved

        @pl.when(inner)
        def _():
            edge_copy(t, 0, OWN, 0, 0, after_pos).wait_send()
            stat_copy(t, 1, 0, after_pos).wait_send()

        @pl.when(inner & jnp.logical_not(here))
        def _():
            edge_copy(t, 1, OWN, 0, 0, after_pos).wait_send()
            stat_copy(t, 2, 0, after_pos).wait_send()

        @pl.when(t > 0)
        def _():
            stat_copy(t, 0, 0, after_pos).wait_send()

        return carry

    lax.fori_loop(0, sweeps + 1, drain, 0)


def run_chain(n, width, chain, table, gate_tile, sites, sketches):
    f32, i32 = jnp.float32, jnp.int32
    count, slots = 2 * n, 2 * STEPS + 1
    vmem = pl.BlockSpec(memory_space=pltpu.VMEM)
    anywhere = pl.BlockSpec(memory_space=pl.ANY)
    dma = pltpu.SemaphoreType.DMA
    return pl.pallas_call(
        functools.partial(chain_kernel, n, width, chain),
        out_shape=(
            jax.ShapeDtypeStruct((2 * count, width, width), f32),
            jax.ShapeDtypeStruct((8, width), f32),
        ),
        in_specs=[vmem, vmem, anywhere, anywhere],
        out_specs=(vmem, vmem),
        scratch_shapes=[
            pltpu.VMEM((2 * count, width, width), f32),
            pltpu.VMEM((count, 2 * width, width), f32),
            pltpu.VMEM((chain, 1, width), i32),
            pltpu.SMEM((chain, 1, width), i32),
            pltpu.VMEM((4, 8, width), f32),
            pltpu.SMEM((4, n), i32),
            pltpu.VMEM((n, 2 * width, width), f32),
            pltpu.VMEM((4, n, 2 * width, width), f32),
            pltpu.VMEM((3, slots + 1, n + 1, 2, width, width), f32),
            pltpu.VMEM((slots + 1, 8, width), f32),
            pltpu.VMEM((3, slots, 8, width), f32),
            pltpu.VMEM((chain, 8, width), f32),
            pltpu.VMEM((8, width), f32),
            pltpu.VMEM((8, width), f32),
            pltpu.VMEM((n + 2, 2 * width, 2 * width), f32),
            pltpu.VMEM((n, 2 * width, width), f32),
            pltpu.VMEM((n, width, width), f32),
            pltpu.VMEM((n, width, width), f32),
            pltpu.VMEM((8, width), f32),
            pltpu.VMEM((8, width), f32),
            dma((3,)),
            dma((chain,)),
            dma((chain,)),
            dma((4,)),
            dma((4,)),
            dma((4,)),
            dma((4,)),
            dma((slots, n)),
            dma((slots, n)),
            dma((n + 1,)),
            dma((n + 1,)),
            dma((slots, 2)),
            dma((slots, 2)),
            dma((slots, 3)),
            dma((slots, 3)),
            dma((chain,)),
            dma((chain,)),
        ],
        compiler_params=pltpu.CompilerParams(
            collective_id=1, has_side_effects=True, vmem_limit_bytes=56 * 1024 * 1024
        ),
    )(table, gate_tile, sites, sketches)


def body(sites, sector_sizes, charge_steps, kept_counts, gates, sketches):
    chain = lax.axis_size("site")
    count, width = sites.shape[2], sites.shape[-1]
    n = count // 2
    table = jnp.concatenate([sector_sizes, kept_counts, charge_steps[:, None]], axis=1)
    table = jnp.pad(table, ((0, 0), (0, width - table.shape[1])))
    gate_tile = jnp.pad(gates, ((0, 7), (0, width - gates.shape[1])))
    out, sums = run_chain(
        n, width, chain, table, gate_tile,
        sites.reshape(2 * count, width, width), sketches.reshape(count, 2 * width, width),
    )
    return out.reshape(sites.shape), sums[:2, 0]


def solution(mesh):
    placed = (
        P("site", None, None, None, None),
        P("site", None),
        P("site"),
        P("site", None),
        P("site", None),
        P("site", None, None, None),
    )
    return jax.shard_map(
        body,
        mesh=mesh,
        in_specs=placed,
        out_specs=(P("site", None, None, None, None), P()),
        check_vma=False,
    )
```

```python
import functools

import jax
import jax.numpy as jnp
from jax import lax
from jax.experimental import pallas as pl
from jax.experimental.pallas import tpu as pltpu
from jax.sharding import PartitionSpec as P

STEPS = 4
HI = lax.Precision.HIGHEST
MESH = pl.DeviceIdType.MESH
OWN, IN, OUT = 0, 1, 2
TAKE, GIVE = (3, 2), (1, 2)


def groups_of(total, sizes):
    out, at = [], 0
    while at < total:
        size = sizes[min(len(out), len(sizes) - 1)]
        out.append(range(at, min(at + size, total)))
        at += size
    return out


def mm(a, b, ca=1, cb=0):
    return lax.dot_general(
        a, b, (((ca,), (cb,)), ((), ())), precision=HI, preferred_element_type=jnp.float32
    )


def split3(a):
    bf16, f32 = jnp.bfloat16, jnp.float32
    a1 = a.astype(bf16)
    rest = a - a1.astype(f32)
    a2 = rest.astype(bf16)
    return a1, a2, (rest - a2.astype(f32)).astype(bf16)


def rank_update(pk, zk, width):
    b1, b2, b3 = split3(jnp.concatenate([pk, zk], axis=1))
    a1, a2, a3 = (b[:, :width] for b in (b1, b2, b3))
    return lax.dot_general(
        jnp.concatenate([a3, a1, a2, a2, a1, a1], axis=0),
        jnp.concatenate([b1, b3, b2, b1, b2, b1], axis=0),
        (((0,), (0,)), ((), ())), preferred_element_type=jnp.float32,
    )


def inverse_factors(w_ref, z_ref, n, width):
    strip, ahead = 32, 4
    lanes = lax.broadcasted_iota(jnp.int32, (1, 8, width), 2)
    subs = lax.broadcasted_iota(jnp.int32, (1, 8, width), 1)
    for b in range(width // strip):
        r0 = b * strip
        groups = strip // 8
        ps = [w_ref[:, r0 + 8 * g : r0 + 8 * g + 8, :] for g in range(groups)]
        if b == 0:
            zs = [
                jnp.broadcast_to((lanes == subs + 8 * g).astype(jnp.float32), ps[0].shape)
                for g in range(groups)
            ]
        else:
            zs = [z_ref[:, r0 + 8 * g : r0 + 8 * g + 8, :] for g in range(groups)]
        for q in range(groups):
            root = jnp.zeros_like(ps[q])
            for h in range(0, 8, ahead):
                c0 = r0 + 8 * q + h
                vs = [
                    [
                        jnp.broadcast_to(ps[g][:, :, c0 + t : c0 + t + 1], ps[g].shape)
                        if g >= q
                        else None
                        for g in range(groups)
                    ]
                    for t in range(ahead)
                ]
                for t in range(ahead):
                    row = h + t
                    piv = vs[t][q][:, row : row + 1, :]
                    inv = lax.rsqrt(piv)
                    inv = inv * (1.5 - 0.5 * piv * inv * inv)
                    inv2 = inv * inv
                    root = jnp.where(subs == row, inv, root)
                    below = jnp.where(subs > row, vs[t][q], 0.0)

                    def eliminate(rows):
                        scaled = rows[q][:, row : row + 1, :] * inv2
                        out = list(rows)
                        if row < 7:
                            out[q] = rows[q] - below * scaled
                        for g in range(q + 1, groups):
                            out[g] = rows[g] - vs[t][g] * scaled
                        return out

                    ps = eliminate(ps)
                    zs = eliminate(zs)
                    for t2 in range(t + 1, ahead):
                        vs[t2] = eliminate(vs[t2])
            ps[q] = ps[q] * root
            zs[q] = zs[q] * root
        for g in range(groups):
            z_ref[:, r0 + 8 * g : r0 + 8 * g + 8, :] = zs[g]
            w_ref[:, r0 + 8 * g : r0 + 8 * g + 8, :] = ps[g]
        r1 = r0 + strip
        if r1 < width:
            rest = width - r1

            def trail(k, carry, r0=r0, r1=r1, rest=rest, b=b):
                both = rank_update(w_ref[k, r0:r1, :], z_ref[k, r0:r1, :], width)[r1:]
                w_ref[k, r1:, :] = w_ref[k, r1:, :] - both[:, :width]
                if b == 0:
                    ri = lax.broadcasted_iota(jnp.int32, (rest, width), 0) + r1
                    ci = lax.broadcasted_iota(jnp.int32, (rest, width), 1)
                    old = (ri == ci).astype(jnp.float32)
                else:
                    old = z_ref[k, r1:, :]
                z_ref[k, r1:, :] = old - both[:, width:]
                return carry

            lax.fori_loop(0, n, trail, 0, unroll=True)


def chain_kernel(
    n, width, chain,
    table, gate_tile, sites, sketches,
    out, sums,
    sites_v, sk_v, tab_v, tab_s, gate_v, kept_s, sk_out, sk_b,
    big, st_own, st_in, all_v, acc, prev_w, mat, smp, w_ref, z_ref, tot, wgt,
    load_sem, bar_send, bar_recv, gate_send, gate_recv, sk_send, sk_recv, tr_send, tr_recv,
    own_send, own_recv,
    ed_send, ed_recv, st_send, st_recv, sum_send, sum_recv,
):
    f32 = jnp.float32
    count = 2 * n
    sweeps = 2 * STEPS
    pos = lax.axis_index("site")

    def place(q):
        return q + lax.rem(q, 2) - lax.rem(lax.div(q, 2), 2) if chain % 4 == 0 else q

    me = place(pos)
    bit = lax.rem(pos, 2)
    home = lax.rem(me, 2)
    moved = lax.rem(bit + home, 2)
    is_moved = moved == 1
    after_pos = lax.rem(pos + 1, chain)
    before_pos = lax.rem(pos + chain - 1, chain)
    before_me = lax.rem(me + chain - 1, chain)
    keeps_next = place(after_pos) == pos

    def even_partner(q):
        return q + 1 - 2 * lax.rem(q, 2)

    def odd_partner(q):
        return lax.rem(q - 1 + 2 * lax.rem(q, 2) + chain, chain)

    load_sites = pltpu.make_async_copy(sites, sites_v, load_sem.at[0])
    load_sk = pltpu.make_async_copy(sketches, sk_v, load_sem.at[1])
    load_sites.start()
    load_sk.start()

    barrier = pltpu.get_barrier_semaphore()

    def greet(off, carry):
        pl.semaphore_signal(
            barrier, inc=1, device_id=(lax.rem(pos + off, chain),), device_id_type=MESH
        )
        return carry

    lax.fori_loop(1, chain, greet, 0)
    pl.semaphore_wait(barrier, chain - 1)

    def remote(src, dst, send, recv, to):
        return pltpu.make_async_remote_copy(
            src_ref=src, dst_ref=dst, send_sem=send, recv_sem=recv,
            device_id=(to,), device_id_type=MESH,
        )

    def table_copy(off):
        return remote(
            table, tab_v.at[pos], bar_send.at[off], bar_recv.at[off], lax.rem(pos + off, chain)
        )

    def begin_table(off, carry):
        table_copy(off).start()
        return carry

    def finish_table(off, carry):
        table_copy(off).wait()
        return carry

    lax.fori_loop(1, chain, begin_table, 0)

    def gate_copy(i, to):
        return remote(gate_tile, gate_v.at[i], gate_send.at[i], gate_recv.at[i], to)

    gate_copy(1, after_pos).start()

    @pl.when(is_moved)
    def _():
        gate_copy(2, me).start()

    @pl.when(jnp.logical_not(keeps_next))
    def _():
        gate_copy(3, place(after_pos)).start()

    tab_v[pos] = table[...]
    gate_v[0] = gate_tile[...]

    @pl.when(jnp.logical_not(is_moved))
    def _():
        gate_v[2] = gate_tile[...]

    @pl.when(keeps_next)
    def _():
        gate_v[3] = gate_tile[...]

    lax.fori_loop(1, chain, finish_table, 0)
    to_scalar = pltpu.make_async_copy(tab_v, tab_s, load_sem.at[2])
    to_scalar.start()
    to_scalar.wait()

    def charge_before(site):
        def add_step(d, total):
            return total + jnp.where(d < site, tab_s[d, 0, 2 * count], 0)

        return lax.rem(lax.fori_loop(0, chain, add_step, jnp.int32(0)), count)

    before = charge_before(pos)
    step = tab_s[pos, 0, 2 * count]
    after = before + step
    me_before = charge_before(me)
    me_after = me_before + tab_s[me, 0, 2 * count]

    def wrap(x):
        return lax.rem(x + 2 * count, count)

    row_ids = lax.broadcasted_iota(jnp.int32, (width, width), 0)
    col_ids = lax.broadcasted_iota(jnp.int32, (width, width), 1)
    col_row = lax.broadcasted_iota(jnp.int32, (1, width), 1)
    eye = row_ids == col_ids

    load_sites.wait()

    def block(charge, p):
        label = wrap(charge - before - bit * p)
        target = wrap(label + p - step)
        rows = tab_s[pos, 0, label]
        cols = tab_s[after_pos, 0, target]
        keep = (row_ids < rows) & (col_ids < cols)
        return jnp.where(keep, sites_v[p * count + label], 0.0)

    theirs = (1 - bit) * n

    def trav_copy(t, k, to):
        return remote(
            big.at[OUT, t, k], big.at[IN, t, k], tr_send.at[t, k], tr_recv.at[t, k], to
        )

    def own_copy(k):
        return remote(
            big.at[OWN, sweeps + 1, k], big.at[OWN, 1, k], own_send.at[k], own_recv.at[k], me
        )

    def edge_copy(t, kind, src, slot, k, to):
        return remote(
            big.at[src, slot, k], big.at[kind, t, n], ed_send.at[t, kind], ed_recv.at[t, kind], to
        )

    def stat_copy(t, kind, slot, to):
        return remote(
            st_own.at[slot], st_in.at[kind, t], st_send.at[t, kind], st_recv.at[t, kind], to
        )

    def own_stat_copy():
        return remote(
            st_own.at[sweeps + 1], st_own.at[1], own_send.at[n], own_recv.at[n], me
        )

    for i in range(n):
        k = n - 1 - i + bit * (2 * i - n + 1)
        for p in range(2):
            big[OUT, 0, k, p] = block(theirs + k, p)
        trav_copy(0, k, even_partner(pos)).start()
    for i in range(n):
        k = n - 1 - i
        for p in range(2):
            big[OWN, 0, k, p] = block(bit * n + k, p)
    last_k = n - 1 - bit * (n - 1)
    for p in range(2):
        big[OWN, 0, n, p] = big[OUT, 0, last_k, p]
    edge_copy(0, 1, OWN, 0, last_k, even_partner(pos)).start()

    load_sk.wait()
    for k in range(n):
        label = wrap(theirs + k - after)
        used = col_row < tab_s[pos, 0, count + label]
        sk_out[k] = jnp.where(used, sk_v[label], 0.0)

    def sk_copy(i, src, to):
        return remote(src, sk_b.at[i], sk_send.at[i], sk_recv.at[i], to)

    @pl.when(bit == 0)
    def _():
        sk_copy(1, sk_out, after_pos).start()

    for k in range(n):
        label = wrap(bit * n + k - after)
        kept = tab_s[pos, 0, count + label]
        used = col_row < kept
        sk_b[0, k] = jnp.where(used, sk_v[label], 0.0)
        kept_s[0, k] = kept
        kept_s[1, k] = tab_s[before_pos, 0, count + wrap(bit * n + k - before)]
        kept_s[2, k] = tab_s[me, 0, count + wrap(home * n + k - me_after)]
        kept_s[3, k] = tab_s[before_me, 0, count + wrap(home * n + k - me_before)]

    @pl.when(is_moved)
    def _():
        sk_copy(2, sk_b.at[0], me).start()

    @pl.when(jnp.logical_not(keeps_next))
    def _():
        sk_copy(3, sk_out, place(after_pos)).start()

    @pl.when(jnp.logical_not(is_moved))
    def _():
        for k in range(n):
            sk_b[2, k] = sk_b[0, k]

    @pl.when(keeps_next)
    def _():
        for k in range(n):
            sk_b[3, k] = sk_out[k]

    gate_copy(1, after_pos).wait()

    @pl.when(is_moved)
    def _():
        gate_copy(2, me).wait()

    @pl.when(jnp.logical_not(keeps_next))
    def _():
        gate_copy(3, place(after_pos)).wait()

    tile_rows = lax.broadcasted_iota(jnp.int32, (8, width), 0)
    ones = jnp.where(tile_rows < 2, 0.5, 0.0)
    st_own[0] = ones
    for kind in range(3):
        st_in[kind, 0] = ones
    acc[...] = jnp.zeros_like(acc)
    prev_w[...] = jnp.ones_like(prev_w)

    def fold_stats(t):
        now = st_own[t] + st_in[0, t]
        total, weight = now[0:1], now[1:2]
        acc[0:1] += 1.0 - weight / total
        acc[1:2] += jnp.log(total) - jnp.log(prev_w[0:1])
        return weight

    def one_sweep(t, carry):
        sweep = lax.rem(t, 2)
        first = 1 - lax.div(t + sweeps - 1, sweeps)
        last = lax.div(t, sweeps - 1)
        q = first * pos + (1 - first) * me
        half = lax.rem(q, 2)
        is_left = half == sweep
        first_moved = (t == 0) & is_moved
        second_moved = (t == 1) & is_moved

        def kk(i):
            return i + half * (n - 1 - 2 * i)

        def jj(m):
            return m + half * (n - 2 * m)

        which = lax.rem(half + sweep, 2)
        left_in, right_in = which, 1 - which
        own_kind = OUT * last * moved
        trav_kind = OUT - own_kind
        own_slot = t + 1 + first * moved * sweeps
        left_out = own_kind + which * (trav_kind - own_kind)
        right_out = OUT - left_out
        left_slot = own_slot + which * (t + 1 - own_slot)
        right_slot = own_slot + t + 1 - left_slot
        table_row = which + 2 * (1 - first)
        idle = (sweep == 1) & ((q == 0) | (q == chain - 1))
        first_edge = sweep

        def left_block(m):
            if m == 0:
                return n - half
            return n - 1 + half if m == n else jj(m) - 1

        ends = last * (moved * me + (1 - moved) * odd_partner(q))
        by = 2 - 4 * lax.rem(q + t, 2)
        travel = ends + (1 - last) * place(lax.rem(q + by + chain, chain))
        even_to = place(even_partner(q))
        odd_to = place(odd_partner(q))

        def send_blocks(group):
            for i in group:
                trav_copy(t + 1, kk(i), travel).start()

            @pl.when(first_moved)
            def _():
                for i in group:
                    own_copy(kk(i)).start()

            if group[0] == 0:
                k = kk(0)

                @pl.when(first_moved)
                def _():
                    for p in range(2):
                        big[IN, 1, n, p] = big[OWN, sweeps + 1, k, p]

                @pl.when((t < sweeps - 1) & jnp.logical_not(first_moved))
                def _():
                    edge_copy(t + 1, 1 - sweep, OUT * sweep, t + 1, k, odd_to).start()

            if group[-1] == n - 1:

                @pl.when(t < sweeps - 1)
                def _():
                    edge_copy(t + 1, sweep, OUT * (1 - sweep), t + 1, kk(n - 1), even_to).start()

        def send_stats():
            near = even_to + sweep * (odd_to - even_to)
            far = odd_to + even_to - near
            stat_copy(t + 1, 0, own_slot, near).start()

            @pl.when(t < sweeps - 1)
            def _():
                stat_copy(t + 1, 1, own_slot, travel).start()

            @pl.when((t < sweeps - 1) & jnp.logical_not(first_moved))
            def _():
                stat_copy(t + 1, 2, own_slot, far).start()

            @pl.when(first_moved)
            def _():
                own_stat_copy().start()
                st_in[2, 1] = st_own[sweeps + 1]

        def wait_blocks(group):
            if group[0] == 0:

                @pl.when((t > 0) & jnp.logical_not(second_moved))
                def _():
                    edge_copy(t, first_edge, OWN, 0, 0, even_to).wait_recv()

            for m in group:
                if m < n:
                    trav_copy(t, kk(m), even_to).wait_recv()

            @pl.when(second_moved)
            def _():
                for m in group:
                    if m < n:
                        own_copy(kk(m)).wait_recv()

            if group[-1] == n:
                edge_copy(t, 1 - first_edge, OWN, 0, 0, even_to).wait_recv()

        def wait_stats():
            @pl.when(t > 0)
            def _():
                for kind in range(2):
                    stat_copy(t, kind, 0, even_to).wait_recv()

            @pl.when((t > 0) & jnp.logical_not(second_moved))
            def _():
                stat_copy(t, 2, 0, even_to).wait_recv()

            @pl.when(second_moved)
            def _():
                own_stat_copy().wait_recv()

            weight = fold_stats(t)
            other = st_in[1, t][1:2] + st_in[2, t][1:2]
            return jnp.where(is_left, weight, other)

        def stats(total, weight):
            st_own[own_slot] = jnp.where(tile_rows == 0, total, jnp.where(tile_rows == 1, weight, 0.0))

        early = (t > 0) & (t < 3)

        @pl.when((t == 0) & (half == 1))
        def _():
            sk_copy(1, sk_out, even_to).wait_recv()

        @pl.when(early & is_left & is_moved)
        def _():
            sk_copy(2, sk_out, even_to).wait_recv()

        @pl.when(early & jnp.logical_not(is_left) & jnp.logical_not(keeps_next))
        def _():
            sk_copy(3, sk_out, even_to).wait_recv()

        @pl.when(idle)
        def _():
            wait_blocks(range(n + 1))
            left_w = wait_stats()
            scale = 1.0 / jnp.sqrt(left_w)
            for i in range(n):
                k = kk(i)
                below = n - 2 * half if i == 0 else n - 2 + 2 * half if i == n - 1 else k - 1
                big[left_out, left_slot, k, 0] = scale * big[left_in, t, k, 0]
                big[left_out, left_slot, k, 1] = scale * big[left_in, t, below, 1]
                big[right_out, right_slot, k, 0] = big[right_in, t, k, 0]
                big[right_out, right_slot, k, 1] = big[right_in, t, k + 1, 1]
            send_blocks(range(n))
            stats(0.5, 0.5)
            send_stats()
            prev_w[...] = jnp.ones_like(prev_w)

        @pl.when(jnp.logical_not(idle))
        def _():
            g = [gate_v[table_row, 0:1, i : i + 1] for i in range(6)]
            tot[...] = jnp.zeros_like(tot)
            wgt[...] = jnp.zeros_like(wgt)

            def mixes(m):
                j = jj(m)
                jl = left_block(m)
                s01 = mm(big[left_in, t, jl, 0], big[right_in, t, j, 1])
                s10 = mm(big[left_in, t, jl, 1], big[right_in, t, j, 0])
                mat[j, :width, width:] = g[2] * s01 + g[3] * s10
                mat[j + 1, width:, :width] = g[4] * s01 + g[5] * s10

            def diagonals(m):
                k = kk(m - 1)
                below = n - 2 * half if m == 1 else n - 2 + 2 * half if m == n else k - 1
                mat[k + 1, :width, :width] = g[0] * mm(
                    big[left_in, t, k, 0], big[right_in, t, k, 0]
                )
                mat[k + 1, width:, width:] = g[1] * mm(
                    big[left_in, t, below, 1], big[right_in, t, k + 1, 1]
                )

            def sample(i):
                k = kk(i)
                mk = mat[k + 1]
                sq = jnp.sum(mk * mk, axis=0, keepdims=True)
                tot[0:1, :] += sq[:, :width] + sq[:, width:]
                smp[k] = mm(mk, sk_b[table_row, k])

            def gram(i):
                k = kk(i)
                s = smp[k]
                w_ref[k] = mm(s, s, 0, 0)

            for group in groups_of(n + 1, TAKE):
                wait_blocks(group)
                for m in group:
                    mixes(m)
                for m in group:
                    if m > 0:
                        diagonals(m)
                for m in group:
                    if m > 0:
                        sample(m - 1)
                for m in group:
                    if m > 0:
                        gram(m - 1)

            left_w = wait_stats()
            for k in range(n):
                s = smp[k]
                used = col_row < kept_s[table_row, k]
                ds = jnp.sum(jnp.sum(s * s, axis=0, keepdims=True), axis=1, keepdims=True)
                kf = kept_s[table_row, k].astype(f32)
                ridge = 0.001 * ds / kf + 1e-06 * left_w
                add = ridge + jnp.where(used, 0.0, 1.0)
                w_ref[k] = w_ref[k] + jnp.where(eye, add, 0.0)
            inverse_factors(w_ref, z_ref, n, width)

            for group in groups_of(n, GIVE):
                reds = []
                for i in group:
                    k = kk(i)
                    basis = mm(smp[k], z_ref[k], 1, 1)
                    for p in range(2):
                        big[left_out, left_slot, k, p] = basis[p * width : (p + 1) * width]
                    reds.append(basis)
                for i, basis in zip(group, reds):
                    k = kk(i)
                    red = mm(basis, mat[k + 1], 0, 0)
                    sq = jnp.sum(red * red, axis=0, keepdims=True)
                    wgt[0:1, :] += sq[:, :width] + sq[:, width:]
                    for p in range(2):
                        big[right_out, right_slot, k, p] = red[:, p * width : (p + 1) * width]
                send_blocks(group)
            stats(
                jnp.sum(tot[0:1, :], axis=1, keepdims=True),
                jnp.sum(wgt[0:1, :], axis=1, keepdims=True),
            )
            send_stats()
            prev_w[...] = jnp.broadcast_to(left_w, prev_w.shape)

        return carry

    lax.fori_loop(0, sweeps, one_sweep, 0)

    stat_copy(sweeps, 0, 0, after_pos).wait_recv()
    weight = fold_stats(sweeps)
    all_v[pos] = 0.5 * acc[...]

    def sum_copy(off):
        return remote(
            all_v.at[pos], all_v.at[pos], sum_send.at[off], sum_recv.at[off],
            lax.rem(pos + off, chain),
        )

    def begin_sum(off, carry):
        sum_copy(off).start()
        return carry

    def finish_sum(off, carry):
        sum_copy(off).wait()
        return carry

    lax.fori_loop(1, chain, begin_sum, 0)
    scale = jnp.where(bit == 1, 1.0, 1.0 / jnp.sqrt(weight))
    for k in range(n):
        trav_copy(sweeps, k, after_pos).wait_recv()
    for p in range(2):
        for l in range(count):
            index = wrap(l + before + bit * p + home * n)
            far = (index >= n).astype(jnp.int32)
            out[p * count + l] = big[far, sweeps, index - n * far, p] * scale
    lax.fori_loop(1, chain, finish_sum, 0)
    sums[...] = jnp.sum(all_v[...], axis=0)

    @pl.when(bit == 0)
    def _():
        sk_copy(1, sk_out, after_pos).wait_send()

    @pl.when(jnp.logical_not(keeps_next))
    def _():
        sk_copy(3, sk_out, after_pos).wait_send()

    @pl.when(is_moved)
    def _():
        sk_copy(2, sk_out, after_pos).wait_send()
        own_stat_copy().wait_send()
        for k in range(n):
            own_copy(k).wait_send()

    edge_copy(0, 1, OWN, 0, 0, after_pos).wait_send()

    def drain(t, carry):
        for k in range(n):
            trav_copy(t, k, after_pos).wait_send()

        inner = (t > 0) & (t < sweeps)
        here = (t == 1) & is_moved

        @pl.when(inner)
        def _():
            edge_copy(t, 0, OWN, 0, 0, after_pos).wait_send()
            stat_copy(t, 1, 0, after_pos).wait_send()

        @pl.when(inner & jnp.logical_not(here))
        def _():
            edge_copy(t, 1, OWN, 0, 0, after_pos).wait_send()
            stat_copy(t, 2, 0, after_pos).wait_send()

        @pl.when(t > 0)
        def _():
            stat_copy(t, 0, 0, after_pos).wait_send()

        return carry

    lax.fori_loop(0, sweeps + 1, drain, 0)


def run_chain(n, width, chain, table, gate_tile, sites, sketches):
    f32, i32 = jnp.float32, jnp.int32
    count, slots = 2 * n, 2 * STEPS + 1
    vmem = pl.BlockSpec(memory_space=pltpu.VMEM)
    anywhere = pl.BlockSpec(memory_space=pl.ANY)
    dma = pltpu.SemaphoreType.DMA
    return pl.pallas_call(
        functools.partial(chain_kernel, n, width, chain),
        out_shape=(
            jax.ShapeDtypeStruct((2 * count, width, width), f32),
            jax.ShapeDtypeStruct((8, width), f32),
        ),
        in_specs=[vmem, vmem, anywhere, anywhere],
        out_specs=(vmem, vmem),
        scratch_shapes=[
            pltpu.VMEM((2 * count, width, width), f32),
            pltpu.VMEM((count, 2 * width, width), f32),
            pltpu.VMEM((chain, 1, width), i32),
            pltpu.SMEM((chain, 1, width), i32),
            pltpu.VMEM((4, 8, width), f32),
            pltpu.SMEM((4, n), i32),
            pltpu.VMEM((n, 2 * width, width), f32),
            pltpu.VMEM((4, n, 2 * width, width), f32),
            pltpu.VMEM((3, slots + 1, n + 1, 2, width, width), f32),
            pltpu.VMEM((slots + 1, 8, width), f32),
            pltpu.VMEM((3, slots, 8, width), f32),
            pltpu.VMEM((chain, 8, width), f32),
            pltpu.VMEM((8, width), f32),
            pltpu.VMEM((8, width), f32),
            pltpu.VMEM((n + 2, 2 * width, 2 * width), f32),
            pltpu.VMEM((n, 2 * width, width), f32),
            pltpu.VMEM((n, width, width), f32),
            pltpu.VMEM((n, width, width), f32),
            pltpu.VMEM((8, width), f32),
            pltpu.VMEM((8, width), f32),
            dma((3,)),
            dma((chain,)),
            dma((chain,)),
            dma((4,)),
            dma((4,)),
            dma((4,)),
            dma((4,)),
            dma((slots, n)),
            dma((slots, n)),
            dma((n + 1,)),
            dma((n + 1,)),
            dma((slots, 2)),
            dma((slots, 2)),
            dma((slots, 3)),
            dma((slots, 3)),
            dma((chain,)),
            dma((chain,)),
        ],
        compiler_params=pltpu.CompilerParams(
            collective_id=1, has_side_effects=True, vmem_limit_bytes=56 * 1024 * 1024
        ),
    )(table, gate_tile, sites, sketches)


def body(sites, sector_sizes, charge_steps, kept_counts, gates, sketches):
    chain = lax.axis_size("site")
    count, width = sites.shape[2], sites.shape[-1]
    n = count // 2
    table = jnp.concatenate([sector_sizes, kept_counts, charge_steps[:, None]], axis=1)
    table = jnp.pad(table, ((0, 0), (0, width - table.shape[1])))
    gate_tile = jnp.pad(gates, ((0, 7), (0, width - gates.shape[1])))
    out, sums = run_chain(
        n, width, chain, table, gate_tile,
        sites.reshape(2 * count, width, width), sketches.reshape(count, 2 * width, width),
    )
    return out.reshape(sites.shape), sums[:2, 0]


def solution(mesh):
    placed = (
        P("site", None, None, None, None),
        P("site", None),
        P("site"),
        P("site", None),
        P("site", None),
        P("site", None, None, None),
    )
    return jax.shard_map(
        body,
        mesh=mesh,
        in_specs=placed,
        out_specs=(P("site", None, None, None, None), P()),
        check_vma=False,
    )
```
